768 devices in a mesh: wave: 48 (over z, x_lo, core), lev: 16 (over x_hi, y).
Axes of the slice: x: 4 (x_hi: 2, x_lo: 2; x = x_hi * 2 + x_lo), y: 8, z: 12, core: 2. Of those that a mesh axis runs over, the one named last changes fastest.
Arguments:
- spectral: bfloat16 [1536, 2, 32, 1536], P('wave', None, 'lev'), may hold values from -6 to 6
- wave_ids: int32 [1536], replicated, may hold values from 0 to 1535, as said below
- lat_rows: int32 [384], replicated, may hold values from 1 to 1152, as said below
- shift_rows: int32 [2, 96, 80], P(None, 'wave', 'lev'), may hold values from -4 to 4, as said below
- shift_cols: int32 [2, 96, 80], P(None, 'wave', 'lev'), may hold values from -4 to 4, as said below
- frac_rows: float32 [2, 96, 80], P(None, 'wave', 'lev'), may hold values from 0 to 1
- frac_cols: float32 [2, 96, 80], P(None, 'wave', 'lev'), may hold values from 0 to 1
- phys_weight: bfloat16 [32, 32], replicated, may hold values from -1 to 1
- phys_bias: float32 [32], replicated, may hold values from -4 to 4
Outputs:
- advected: bfloat16 [32, 384, 10240], P(None, 'wave', 'lev')
The draws below stay inside these ranges and needn't reach their ends.
Inputs may be any that keep to these rules, and one draw needn't show every extreme that they name: wave_ids: a permutation of the wavenumbers; slot r lies on the wave device of index r // 32. lat_rows: strictly increasing; row j lies at colatitude pi * lat_rows[j] / 1536, so the window covers colatitudes up to some 135 degrees. shift_rows: both the smallest and the largest value occur in every draw. shift_cols: both the smallest and the largest value occur in every draw.
All inputs are finite; a program needn't handle non-finite values.
Results may differ from the reference program's by a relative error of at most 0.005.
Values may be sent and summed in bfloat16 or wider, within the bound.
No kernel may reach another device: no remote copies, remote signals or barrier semaphores. Data moves between devices by JAX's collectives and lax.ppermute only.
A program may use at most 32 MiB of HBM per device.

```python
import math
import jax
import jax.numpy as jnp
from jax import lax

M = 1536
NLON = 10240
STEPS = 2
MAX_SHIFT = 4
BLOCK_ROWS = 4
BLOCK_COLS = 128
RIM_WIDTH = 6
F = 32
LAT = 384


def draw_wave_ids(key, part):
    base = jnp.arange(M, dtype=jnp.int32)
    jitter = jax.random.randint(jax.random.fold_in(key, 11), (M,), 0, max(M // 4, 2), dtype=jnp.int32)
    scores = (base + jitter) * M + base
    return jnp.argsort(scores, stable=True).astype(jnp.int32)


def draw_lat_rows(key, part):
    offsets = jax.random.randint(jax.random.fold_in(key, 12), (LAT,), 1, 4, dtype=jnp.int32)
    offsets = offsets.at[0].set(1).at[LAT - 1].set(3)
    return 3 * jnp.arange(LAT, dtype=jnp.int32) + offsets


def shift_draw(key, salt):
    total = STEPS * (LAT // BLOCK_ROWS) * (NLON // BLOCK_COLS)
    values = jax.random.randint(jax.random.fold_in(key, salt), (total,), -MAX_SHIFT, MAX_SHIFT + 1, dtype=jnp.int32)
    first_place = jax.random.randint(jax.random.fold_in(key, salt + 1), (), 0, total, dtype=jnp.int32)
    place_gap = jax.random.randint(jax.random.fold_in(key, salt + 2), (), 1, total, dtype=jnp.int32)
    second_place = (first_place + place_gap) % total
    values = values.at[first_place].set(MAX_SHIFT).at[second_place].set(-MAX_SHIFT)
    return values.reshape(STEPS, LAT // BLOCK_ROWS, NLON // BLOCK_COLS)


def draw_shift_rows(key, part):
    return shift_draw(key, 21)


def draw_shift_cols(key, part):
    return shift_draw(key, 31)


def block_levels(rng, dims, pieces, low, largest):
    factor_of = 1.0
    for position, parts in pieces:
        draws = jax.random.uniform(jax.random.fold_in(jax.random.fold_in(rng, 6), position), (parts,), jnp.float32, low / len(pieces), largest / len(pieces))
        factor_of = factor_of * jnp.repeat(jnp.exp(draws), dims[position] // parts).reshape((-1,) + (1,) * (len(dims) - 1 - position))
    return factor_of


def gaussian(key, shape, spread, most, cuts=(), kind=jnp.bfloat16):
    loudness = block_levels(key, shape, cuts, -0.22, 0.18) if cuts else 1.0
    values = jax.random.normal(key, shape, jnp.float32) * spread * loudness
    return jnp.minimum(jnp.maximum(values, -most), most).astype(kind)


def setup_inputs(seed: int = 0) -> dict:
    streams_of = jax.random.split(jax.random.key(seed), 10)
    spectral = gaussian(streams_of[0], (M, 2, F, M), 1.0, 6.0, ((0, 48), (2, 16)))
    wave_ids = draw_wave_ids(jax.random.fold_in(streams_of[9], 71), 0)
    lat_rows = draw_lat_rows(jax.random.fold_in(streams_of[9], 71), 0)
    shift_rows = draw_shift_rows(jax.random.fold_in(streams_of[9], 71), 0)
    shift_cols = draw_shift_cols(jax.random.fold_in(streams_of[9], 71), 0)
    frac_rows = jnp.clip(1.0 * jax.random.uniform(streams_of[5], (STEPS, LAT // BLOCK_ROWS, NLON // BLOCK_COLS), jnp.float32) ** block_levels(streams_of[5], (STEPS, LAT // BLOCK_ROWS, NLON // BLOCK_COLS), ((1, 48), (2, 16)), -0.2, 0.2), 0.0, 1.0)
    frac_cols = jnp.clip(1.0 * jax.random.uniform(streams_of[6], (STEPS, LAT // BLOCK_ROWS, NLON // BLOCK_COLS), jnp.float32) ** block_levels(streams_of[6], (STEPS, LAT // BLOCK_ROWS, NLON // BLOCK_COLS), ((1, 48), (2, 16)), -0.2, 0.2), 0.0, 1.0)
    phys_weight = gaussian(streams_of[7], (F, F), F ** -0.5, 1.0)
    phys_bias = gaussian(streams_of[8], (F,), 1.0, 4.0, (), jnp.float32)
    return {"spectral": spectral, "wave_ids": wave_ids, "lat_rows": lat_rows, "shift_rows": shift_rows, "shift_cols": shift_cols, "frac_rows": frac_rows, "frac_cols": frac_cols, "phys_weight": phys_weight, "phys_bias": phys_bias}


def angle_pair(first_ints, second_ints, period):
    product = first_ints[:, None] * second_ints[None, :] % period
    angles = product.astype(jnp.float32) * (2.0 * math.pi / period)
    return (jnp.cos(angles), jnp.sin(angles))

def cubic_weights(fraction):
    coord = 1.0 - fraction
    return (-coord * (coord - 1.0) * (coord - 2.0) / 6.0, (coord + 1.0) * (coord - 1.0) * (coord - 2.0) / 2.0, -(coord + 1.0) * coord * (coord - 2.0) / 2.0, (coord + 1.0) * coord * (coord - 1.0) / 6.0)

def interpolate(window, row_frac, col_frac):
    window = window.astype(jnp.float32)
    row_weights = cubic_weights(row_frac)
    col_weights = cubic_weights(col_frac)
    along = row_weights[0] * window[:, 0:BLOCK_ROWS]
    along = along + row_weights[1] * window[:, 1:BLOCK_ROWS + 1]
    along = along + row_weights[2] * window[:, 2:BLOCK_ROWS + 2]
    along = along + row_weights[3] * window[:, 3:BLOCK_ROWS + 3]
    result = col_weights[0] * along[:, :, 0:BLOCK_COLS]
    result = result + col_weights[1] * along[:, :, 1:BLOCK_COLS + 1]
    result = result + col_weights[2] * along[:, :, 2:BLOCK_COLS + 2]
    result = result + col_weights[3] * along[:, :, 3:BLOCK_COLS + 3]
    return result

def column_physics(departed, phys_weight, phys_bias):
    flat = departed.reshape(departed.shape[0], -1)
    forcing = jnp.dot(phys_weight, flat.astype(jnp.bfloat16), preferred_element_type=jnp.float32) + phys_bias[:, None]
    return (flat + jnp.tanh(forcing)).astype(jnp.bfloat16).reshape(departed.shape)

def block_update(padded, row_start, col_start, row_move, col_move, row_part, col_part, phys_weight, phys_bias):
    lead_rows = RIM_WIDTH - 2
    window = lax.dynamic_slice(padded, (jnp.int32(0), row_start + lead_rows - row_move, col_start + lead_rows - col_move), (padded.shape[0], BLOCK_ROWS + 3, BLOCK_COLS + 3))
    return column_physics(interpolate(window, row_part, col_part), phys_weight, phys_bias)

def substep(field_state, row_shift, col_shift, row_frac, col_frac, phys_weight, phys_bias):
    padded = jnp.pad(field_state, ((0, 0), (RIM_WIDTH, RIM_WIDTH), (0, 0)))
    padded = jnp.concatenate([padded[:, :, -RIM_WIDTH:], padded, padded[:, :, :RIM_WIDTH]], axis=2)
    row_starts = jnp.arange(row_shift.shape[0], dtype=jnp.int32) * BLOCK_ROWS
    col_starts = jnp.arange(row_shift.shape[1], dtype=jnp.int32) * BLOCK_COLS

    def row_block(operands):
        row_start, moves_r, moves_c, parts_r, parts_c = operands

        def one_block(col_start, row_move, col_move, row_part, col_part):
            return block_update(padded, row_start, col_start, row_move, col_move, row_part, col_part, phys_weight, phys_bias)
        return jax.vmap(one_block)(col_starts, moves_r, moves_c, parts_r, parts_c)
    blocks = lax.map(row_block, (row_starts, row_shift, col_shift, row_frac, col_frac))
    return blocks.transpose(2, 0, 3, 1, 4).reshape(field_state.shape[0], row_shift.shape[0] * BLOCK_ROWS, row_shift.shape[1] * BLOCK_COLS)

def reference(spectral, wave_ids, lat_rows, shift_rows, shift_cols, frac_rows, frac_cols, phys_weight, phys_bias):
    k_index = jnp.arange(M, dtype=jnp.int32)
    keep_mask = k_index[None, :] < (M - wave_ids)[:, None]
    coefficients = jnp.where(keep_mask[:, None, None, :], spectral, jnp.zeros_like(spectral))
    cos_k, sin_k = angle_pair(k_index, lat_rows, 8 * LAT)
    basis_table = jnp.concatenate([cos_k, sin_k], axis=1).astype(jnp.bfloat16)
    cos_wave, sin_wave = angle_pair(wave_ids, lat_rows, 8 * LAT)
    scale_factor = 1.0 / math.sqrt(M)

    def one_slot(operands):
        coeffs, cos_row, sin_row = operands
        projected = jnp.dot(coeffs.reshape(-1, M), basis_table, preferred_element_type=jnp.float32)
        projected = projected.reshape(coeffs.shape[0], coeffs.shape[1], 2, LAT)
        return ((cos_row * projected[:, :, 0] - sin_row * projected[:, :, 1]) * scale_factor).astype(jnp.bfloat16)
    legendre = lax.map(one_slot, (coefficients, cos_wave, sin_wave))
    lon_index = jnp.arange(NLON, dtype=jnp.int32)
    cos_lon, sin_lon = angle_pair(wave_ids, lon_index, NLON)
    fourier_table = jnp.stack([cos_lon, -sin_lon], axis=1).astype(jnp.bfloat16)

    def one_row(coeffs):
        summed = lax.dot_general(coeffs, fourier_table, (((0, 1), (0, 1)), ((), ())), preferred_element_type=jnp.float32)
        return (summed * scale_factor).astype(jnp.bfloat16)
    rows_out = lax.map(one_row, legendre.transpose(3, 0, 1, 2))
    field_state = rows_out.transpose(1, 0, 2)
    for substep_index in range(STEPS):
        field_state = substep(field_state, shift_rows[substep_index], shift_cols[substep_index], frac_rows[substep_index], frac_cols[substep_index], phys_weight, phys_bias)
    return field_state
```

```python
import functools
import math

import jax
import jax.numpy as jnp
from jax import lax
from jax.experimental import pallas as pl
from jax.experimental.pallas import tpu as pltpu
from jax.sharding import PartitionSpec as P

BLOCK_ROWS = 4
BLOCK_COLS = 128
LANES = 128
ABOVE = 6
BELOW = 5
STAMP_LANE = 32
F32 = jnp.float32
BF16 = jnp.bfloat16
NT = (((1,), (1,)), ((), ()))


def sincos(x, period):
    quarter = period // 4
    turns = jnp.floor(x * (1.0 / quarter) + 0.5)
    t = (x - turns * float(quarter)) * (2.0 * math.pi / period)
    t2 = t * t
    s = t * (1.0 + t2 * (-1.0 / 6.0 + t2 * (1.0 / 120.0 + t2 * (-1.0 / 5040.0))))
    c = 1.0 + t2 * (-0.5 + t2 * (1.0 / 24.0 + t2 * (-1.0 / 720.0 + t2 * (1.0 / 40320.0))))
    k = turns.astype(jnp.int32)
    swap = (k & 1) == 1
    cos, sin = jnp.where(swap, s, c), jnp.where(swap, c, s)
    cos = jnp.where(((k + 1) & 2) != 0, -cos, cos)
    sin = jnp.where((k & 2) != 0, -sin, sin)
    return cos, sin


def rotate(c, s, rc, rs):
    return c * rc - s * rs, s * rc + c * rs


def legendre_kernel(period, scale, x_ref, m_col_ref, m_row_ref, lat_ref, out_ref, cos_ref, sin_ref, cw_ref, sw_ref):
    rows, waves = x_ref.shape
    lats = lat_ref.shape[0]
    step = 32
    lane = lax.broadcasted_iota(jnp.int32, (step, LANES), 1).astype(F32)
    m_row = jnp.broadcast_to(m_row_ref[...], (step, LANES))

    def fill(i, carry):
        at = pl.ds(pl.multiple_of(i * step, step), step)
        lat = jnp.broadcast_to(lat_ref[at, :], (step, LANES))
        cw, sw = sincos(lat * m_row, period)
        cw_ref[at, :] = cw
        sw_ref[at, :] = sw
        c, s = sincos(lat * lane, period)
        rc, rs = sincos(lat * float(LANES), period)
        for a in range(waves // LANES):
            cols = pl.ds(a * LANES, LANES)
            cos_ref[at, cols] = c.astype(BF16)
            sin_ref[at, cols] = s.astype(BF16)
            if a + 1 < waves // LANES:
                c, s = rotate(c, s, rc, rs)
        return carry

    lax.fori_loop(0, lats // step, fill, 0)
    k = lax.broadcasted_iota(jnp.int32, (rows, waves), 1)
    x = jnp.where(k < waves - m_col_ref[...], x_ref[...].astype(F32), 0.0).astype(BF16)
    p0 = lax.dot_general(cos_ref[...], x, NT, preferred_element_type=F32)
    p1 = lax.dot_general(sin_ref[...], x, NT, preferred_element_type=F32)
    leg = ((cw_ref[...] * p0 - sw_ref[...] * p1) * scale).astype(BF16)
    src = lax.broadcasted_iota(jnp.int32, (rows, rows), 0)
    dst = lax.broadcasted_iota(jnp.int32, (rows, rows), 1)
    slots = rows // 4
    order = jnp.where((src % 4) * slots + src // 4 == dst, 1.0, 0.0).astype(BF16)
    out_ref[...] = jnp.dot(leg, order, preferred_element_type=F32).astype(BF16)


def legendre(x, own_ids, lat_rows, period, scale):
    rows, waves = x.shape
    lats = lat_rows.shape[0]
    ids = jnp.repeat(own_ids, 4)
    return pl.pallas_call(
        functools.partial(legendre_kernel, period, scale),
        out_shape=jax.ShapeDtypeStruct((lats, rows), BF16),
        scratch_shapes=[
            pltpu.VMEM((lats, waves), BF16),
            pltpu.VMEM((lats, waves), BF16),
            pltpu.VMEM((lats, LANES), F32),
            pltpu.VMEM((lats, LANES), F32),
        ],
        compiler_params=pltpu.CompilerParams(vmem_limit_bytes=24 << 20),
        name="legendre",
    )(x, ids[:, None], ids[None, :].astype(F32), lat_rows.astype(F32)[:, None])


def times_i(z, power):
    re, im = z
    return ((re, im), (-im, re), (-re, -im), (im, -re))[power % 4]


def add(*terms):
    re, im = terms[0]
    for r, i in terms[1:]:
        re, im = re + r, im + i
    return re, im


def four(z):
    a, b = add(z[0], z[2]), add(z[0], times_i(z[2], 2))
    c, d = add(z[1], z[3]), add(z[1], times_i(z[3], 2))
    return add(a, c), add(b, times_i(d, 1)), add(a, times_i(c, 2)), add(b, times_i(d, 3))


def sixteen_real(y):
    inner = [four([y[4 * q1 + q0] for q1 in range(4)]) for q0 in range(4)]
    out = [None] * 16
    for a0 in range(4):
        v = []
        for q0 in range(4):
            re, im = inner[q0][a0]
            if q0 * a0:
                angle = 2.0 * math.pi * q0 * a0 / 16.0
                cos, sin = math.cos(angle), math.sin(angle)
                re, im = re * cos - im * sin, re * sin + im * cos
            v.append((re, im))
        even, odd = v[0][0] + v[2][0], v[0][0] - v[2][0]
        plus, minus = v[1][0] + v[3][0], v[3][1] - v[1][1]
        out[a0], out[a0 + 8] = even + plus, even - plus
        out[a0 + 4], out[a0 + 12] = odd + minus, odd - minus
    return out


def fourier_kernel(nlon, scale, z_ref, m_ref, stamp_ref, out_ref, e_ref, l_ref, d_ref):
    waves = m_ref.shape[1]
    chunks = waves // LANES
    spans = e_ref.shape[0] // 64
    sub = lax.broadcasted_iota(jnp.int32, (8, LANES), 0).astype(F32)

    def table(i, carry):
        at = pl.ds(pl.multiple_of(i * LANES, LANES), LANES)
        at_sin = pl.ds(pl.multiple_of(waves + i * LANES, LANES), LANES)
        m = jnp.broadcast_to(m_ref[:, at], (8, LANES))
        c, s = sincos(m * sub, nlon)
        c8, s8 = sincos(m * 8.0, nlon)
        c64, s64 = sincos(m * 64.0, nlon)
        z = [(c, s)]
        for _ in range(7):
            z.append(rotate(*z[-1], c8, s8))
        start = z
        for t in range(spans):
            if t == spans - 1:
                z = [rotate(a, b, c64, -s64) for a, b in start]
            for h in range(4):
                (c0, s0), (c1, s1) = z[2 * h], z[2 * h + 1]
                rows = pl.ds(t * 64 + h * 16, 16)
                e_ref[rows, at] = jnp.concatenate([c0, c1], axis=0).astype(BF16)
                e_ref[rows, at_sin] = jnp.concatenate([s0, s1], axis=0).astype(BF16)
            if t < spans - 2:
                z = [rotate(a, b, c64, s64) for a, b in z]
        return carry

    lax.fori_loop(0, chunks, table, 0)
    group = lax.broadcasted_iota(jnp.int32, (8, LANES), 1) // 32

    def spread(i, carry):
        at = pl.ds(pl.multiple_of(i * LANES, LANES), LANES)
        at_sin = pl.ds(pl.multiple_of(waves + i * LANES, LANES), LANES)
        block = [z_ref[4 * i + u].astype(F32) for u in range(4)]
        parts = []
        for cf in range(4):
            whole = None
            for u in range(4):
                turn = (32 * (u - cf)) % LANES
                moved = pltpu.roll(block[u], turn, 1) if turn else block[u]
                whole = moved if whole is None else jnp.where(group == u, moved, whole)
            parts.append(whole)
        real = jnp.concatenate(parts[0:2], axis=0)
        imag = jnp.concatenate(parts[2:4], axis=0)
        m = jnp.broadcast_to(m_ref[:, at], (16, LANES))
        residue = m - 16.0 * jnp.floor(m * 0.0625)
        for q in range(16):
            keep = residue == float(q)
            re = jnp.where(keep, real, 0.0)
            im = jnp.where(keep, imag, 0.0)
            top, low = pl.ds(q * 32, 16), pl.ds(q * 32 + 16, 16)
            re16, im16 = re.astype(BF16), im.astype(BF16)
            l_ref[top, at] = re16
            l_ref[low, at] = im16
            l_ref[top, at_sin] = (-im).astype(BF16)
            l_ref[low, at_sin] = re16
        return carry

    lax.fori_loop(0, chunks, spread, 0)
    lane = lax.broadcasted_iota(jnp.int32, (16, LANES), 1)
    unused = (lane >= STAMP_LANE) & (lane < LANES - STAMP_LANE)
    stamp = jnp.broadcast_to(stamp_ref[...], (16, LANES))
    tiles = e_ref.shape[0] // LANES
    for pair in range(tiles // 2):
        d_ref[...] = lax.dot_general(
            l_ref[...], e_ref[pl.ds(pair * 256, 256), :], NT, preferred_element_type=F32
        )
        for h in range(2):
            t = 2 * pair + h
            cols = pl.ds(h * LANES, LANES)
            y = [(d_ref[pl.ds(q * 32, 16), cols], d_ref[pl.ds(q * 32 + 16, 16), cols]) for q in range(16)]
            g = sixteen_real(y)
            for a in range(16):
                value = g[a] * scale
                if t == tiles - 1:
                    value = jnp.where(unused, stamp, value)
                out_ref[a, pl.ds(t * 16, 16), :] = value.astype(BF16)


def fourier(z, wave_ids, stamp, nlon, scale):
    waves = wave_ids.shape[0]
    tiles = 6
    return pl.pallas_call(
        functools.partial(fourier_kernel, nlon, scale),
        out_shape=jax.ShapeDtypeStruct((16, tiles * 16, LANES), BF16),
        scratch_shapes=[
            pltpu.VMEM((tiles * LANES, 2 * waves), BF16),
            pltpu.VMEM((512, 2 * waves), BF16),
            pltpu.VMEM((512, 256), F32),
        ],
        compiler_params=pltpu.CompilerParams(vmem_limit_bytes=24 << 20),
        name="fourier",
    )(z, wave_ids.astype(F32)[None, :], stamp)


def regroup_kernel(x_ref, out_ref, wide_ref):
    rows, tiles = out_ref.shape[:2]
    sources = x_ref.shape[0]
    span = x_ref.shape[1]
    for v in range(sources):
        wide_ref[pl.ds(v * span, span), :] = x_ref[v].astype(F32)
    for j in range(rows):
        for t in range(tiles):
            for f in range(2):
                got = wide_ref[pl.ds(t * 16 + f * 8 + j, sources, stride=span), :]
                out_ref[j, t, pl.ds(f * sources, sources), :] = got.astype(BF16)


def regroup(x):
    return pl.pallas_call(
        regroup_kernel,
        out_shape=jax.ShapeDtypeStruct((8, x.shape[1] // 16, 32, LANES), BF16),
        scratch_shapes=[pltpu.VMEM((x.shape[0] * x.shape[1], LANES), F32)],
        compiler_params=pltpu.CompilerParams(vmem_limit_bytes=8 << 20),
        name="regroup",
    )(x)


def advance_kernel(last, move_ref, weight_ref, before_ref, now_ref, after_ref, phys_ref, bias_ref, out_ref, s_ref, *rest):
    rows, tiles, fields = now_ref.shape[:3]
    s_ref[pl.ds(0, ABOVE)] = before_ref[...]
    s_ref[pl.ds(ABOVE, rows)] = now_ref[...]
    s_ref[pl.ds(ABOVE + rows, BELOW)] = after_ref[...]
    lane = lax.broadcasted_iota(jnp.int32, (fields, LANES), 1)
    left_half = lane < LANES // 2
    phys = phys_ref[...]
    bias = jnp.broadcast_to(bias_ref[...], (fields, LANES))

    def departed(band, block, tile):
        where = band * 7 + block
        base = ABOVE - 2 + band * BLOCK_ROWS - move_ref[2 * where]
        first = -move_ref[2 * where + 1] - 2
        wr = [weight_ref[8 * where + a] for a in range(4)]
        wc = [weight_ref[8 * where + 4 + a] for a in range(4)]
        centre, edge = [], []
        for k in range(BLOCK_ROWS + 3):
            before = s_ref[base + k, (tile + tiles - 1) % tiles].astype(F32)
            after = s_ref[base + k, (tile + 1) % tiles].astype(F32)
            centre.append(s_ref[base + k, tile].astype(F32))
            edge.append(jnp.where(left_half, after, before))
        taps = []
        for b in range(4):
            shift = first + b
            outside = (lane < shift) | (lane >= LANES + shift)
            taps.append((outside, (LANES - shift) & (LANES - 1)))
        result = []
        for i in range(BLOCK_ROWS):
            c = sum(wr[a] * centre[i + a] for a in range(4))
            e = sum(wr[a] * edge[i + a] for a in range(4))
            total = None
            for b in range(4):
                outside, turn = taps[b]
                term = wc[b] * pltpu.roll(jnp.where(outside, e, c), turn, 1)
                total = term if total is None else total + term
            result.append(total)
        return result

    def one_band(band, carry):
        for tile in range(5 if last else 6):
            if tile < 5:
                dep = departed(band, tile + 1, tile)
            else:
                right = departed(band, 6, tile)
                left = departed(band, 0, tile)
                dep = [jnp.where(left_half, r, l) for r, l in zip(right, left)]
            low = jnp.concatenate(dep, axis=1).astype(BF16)
            forcing = jnp.dot(phys, low, preferred_element_type=F32)
            for i in range(BLOCK_ROWS):
                push = forcing[:, i * LANES : (i + 1) * LANES] + bias
                value = dep[i] + jnp.tanh(push)
                row = band * BLOCK_ROWS + i
                if last:
                    at = pl.ds(pl.multiple_of((row * 5 + tile) * fields, fields), fields)
                    rest[0][at, :] = value
                else:
                    out_ref[row, tile] = value.astype(BF16)
        return carry

    lax.fori_loop(0, rows // BLOCK_ROWS, one_band, 0)
    if last:
        for f in range(fields):
            kept = (f % 2) * (fields // 2) + f // 2
            for t in range(5):
                got = rest[0][pl.ds(t * fields + kept, rows, stride=5 * fields), :]
                out_ref[f, :, pl.ds(t * LANES, LANES)] = got.astype(BF16)


def advance(last, moves, weights, before, now, after, phys, bias):
    rows, tiles, fields = now.shape[:3]
    smem, vmem = pl.BlockSpec(memory_space=pltpu.SMEM), pl.BlockSpec(memory_space=pltpu.VMEM)
    scratch = [pltpu.VMEM((ABOVE + rows + BELOW, tiles, fields, LANES), BF16)]
    if last:
        shape = (fields, rows, 5 * LANES)
        scratch.append(pltpu.VMEM((rows * 5 * fields, LANES), F32))
    else:
        shape = (rows, tiles, fields, LANES)
    return pl.pallas_call(
        functools.partial(advance_kernel, last),
        out_shape=jax.ShapeDtypeStruct(shape, BF16),
        in_specs=[smem, smem] + [vmem] * 5,
        scratch_shapes=scratch,
        compiler_params=pltpu.CompilerParams(vmem_limit_bytes=16 << 20),
        name="advance_last" if last else "advance_first",
    )(moves, weights, before, now, after, phys, bias)


def cubic_weights(fraction):
    coord = 1.0 - fraction
    return (
        -coord * (coord - 1.0) * (coord - 2.0) / 6.0,
        (coord + 1.0) * (coord - 1.0) * (coord - 2.0) / 2.0,
        -(coord + 1.0) * coord * (coord - 2.0) / 2.0,
        (coord + 1.0) * coord * (coord - 1.0) / 6.0,
    )


def three_parts(value):
    high = lax.reduce_precision(value, 8, 7)
    mid = lax.reduce_precision(value - high, 8, 7)
    return high, mid, value - high - mid


def edge_stamp(shift_rows, shift_cols, frac_rows, frac_cols):
    pieces = [shift_rows.astype(F32), shift_cols.astype(F32), *three_parts(frac_rows), *three_parts(frac_cols)]
    table = jnp.stack(pieces, axis=0)
    edges = jnp.concatenate([table[:, :, :1], table[:, :, -1:]], axis=2)
    flat = edges.reshape(1, -1)
    return jnp.pad(flat, ((0, 0), (STAMP_LANE, LANES - STAMP_LANE - flat.shape[1])))


def read_stamp(lanes, side):
    table = lanes.astype(F32).reshape(8, 2, 2)[:, :, side : side + 1]
    return table[0], table[1], table[2] + table[3] + table[4], table[5] + table[6] + table[7]


def block_tables(shift_rows, shift_cols, frac_rows, frac_cols):
    moves = jnp.stack([shift_rows, shift_cols], axis=-1).astype(jnp.int32).reshape(-1)
    weights = jnp.stack(cubic_weights(frac_rows) + cubic_weights(frac_cols), axis=-1).reshape(-1)
    return moves, weights


def row_halos(state):
    size = lax.axis_size("wave")
    rows = state.shape[0]
    before = lax.ppermute(state[rows - ABOVE :], "wave", [(i, i + 1) for i in range(size - 1)])
    after = lax.ppermute(state[:BELOW], "wave", [(i + 1, i) for i in range(size - 1)])
    return before, after


def shards(spectral, wave_ids, lat_rows, shift_rows, shift_cols, frac_rows, frac_cols, phys_weight, phys_bias):
    slots, parts, fields, waves = spectral.shape
    lats = lat_rows.shape[0]
    bands, owners = lax.axis_size("wave"), lax.axis_size("lev")
    nlon = shift_rows.shape[2] * BLOCK_COLS * owners
    scale = 1.0 / math.sqrt(waves)
    own_ids = lax.dynamic_slice_in_dim(wave_ids, lax.axis_index("wave") * slots, slots)
    outgoing = legendre(spectral.reshape(slots * parts * fields, waves), own_ids, lat_rows, 8 * lats, scale)
    outgoing = outgoing.reshape(bands, lats // bands, slots * parts * fields)
    arrived = lax.all_to_all(outgoing, "wave", split_axis=0, concat_axis=0, tiled=True)
    stamp = edge_stamp(shift_rows[0], shift_cols[0], frac_rows[0], frac_cols[0])
    columns = fourier(arrived, wave_ids, stamp, nlon, scale)
    columns = lax.all_to_all(columns, "lev", split_axis=0, concat_axis=0, tiled=True)
    state = regroup(columns)
    before, after = row_halos(state)

    me = lax.axis_index("lev")
    stamp_row = columns.shape[1] - 16
    size = (1, 1, 32)
    west = lax.dynamic_slice(columns, ((me + owners - 1) % owners, stamp_row, STAMP_LANE), size)
    east = lax.dynamic_slice(columns, ((me + 1) % owners, stamp_row, STAMP_LANE), size)
    west, east = read_stamp(west, 1), read_stamp(east, 0)
    own = (shift_rows.astype(F32), shift_cols.astype(F32), frac_rows, frac_cols)
    first = [jnp.concatenate([w, o[0], e], axis=1) for w, o, e in zip(west, own, east)]
    second = [jnp.pad(o[1], ((0, 0), (1, 1))) for o in own]

    split = (owners, fields)
    phys = phys_weight.reshape(split + split).transpose(1, 0, 3, 2).reshape(phys_weight.shape)
    bias = phys_bias.reshape(split).T.reshape(-1, 1)
    state = advance(False, *block_tables(*first), before, state, after, phys, bias)
    before, after = row_halos(state)
    return advance(True, *block_tables(*second), before, state, after, phys, bias)


def solution(mesh):
    blocks = P(None, "wave", "lev")
    return jax.shard_map(
        shards,
        mesh=mesh,
        in_specs=(P("wave", None, "lev", None), P(), P(), blocks, blocks, blocks, blocks, P(), P()),
        out_specs=P(None, "wave", "lev"),
        check_vma=False,
    )
```

```python
import functools
import math

import jax
import jax.numpy as jnp
from jax import lax
from jax.experimental import pallas as pl
from jax.experimental.pallas import tpu as pltpu
from jax.sharding import PartitionSpec as P

BLOCK_ROWS = 4
BLOCK_COLS = 128
LANES = 128
ABOVE = 6
BELOW = 5
STAMP_LANE = 32
F32 = jnp.float32
BF16 = jnp.bfloat16
NT = (((1,), (1,)), ((), ()))


def sincos(x, period):
    quarter = period // 4
    turns = jnp.floor(x * (1.0 / quarter) + 0.5)
    t = (x - turns * float(quarter)) * (2.0 * math.pi / period)
    t2 = t * t
    s = t * (1.0 + t2 * (-1.0 / 6.0 + t2 * (1.0 / 120.0 + t2 * (-1.0 / 5040.0))))
    c = 1.0 + t2 * (-0.5 + t2 * (1.0 / 24.0 + t2 * (-1.0 / 720.0 + t2 * (1.0 / 40320.0))))
    k = turns.astype(jnp.int32)
    swap = (k & 1) == 1
    cos, sin = jnp.where(swap, s, c), jnp.where(swap, c, s)
    cos = jnp.where(((k + 1) & 2) != 0, -cos, cos)
    sin = jnp.where((k & 2) != 0, -sin, sin)
    return cos, sin


def rotate(c, s, rc, rs):
    return c * rc - s * rs, s * rc + c * rs


def legendre_kernel(period, middle, turn, scale, x_ref, m_col_ref, m_row_ref, lat_ref, out_ref, cos_ref, sin_ref, cw_ref, sw_ref):
    rows, waves = x_ref.shape
    lats = lat_ref.shape[0]
    step = 32
    lane = lax.broadcasted_iota(jnp.int32, (step, LANES), 1).astype(F32)
    m_row = jnp.broadcast_to(m_row_ref[...], (step, LANES))

    def fill(i, carry):
        at = pl.ds(pl.multiple_of(i * step, step), step)
        lat = jnp.broadcast_to(lat_ref[at, :], (step, LANES))
        cw, sw = sincos(lat * m_row, period)
        cw_ref[at, :] = cw
        sw_ref[at, :] = sw
        c, s = sincos(lat * lane, period)
        rc, rs = sincos(lat * float(LANES), period)
        for a in range(waves // LANES):
            cols = pl.ds(a * LANES, LANES)
            cos_ref[at, cols] = c.astype(BF16)
            sin_ref[at, cols] = s.astype(BF16)
            if a + 1 < waves // LANES:
                c, s = rotate(c, s, rc, rs)
        return carry

    lax.fori_loop(0, lats // step, fill, 0)
    k = lax.broadcasted_iota(jnp.int32, (rows, waves), 1)
    x = jnp.where(k < waves - m_col_ref[...], x_ref[...].astype(F32), 0.0).astype(BF16)
    p0 = lax.dot_general(cos_ref[...], x, NT, preferred_element_type=F32)
    p1 = lax.dot_general(sin_ref[...], x, NT, preferred_element_type=F32)
    leg = (cw_ref[...] * p0 - sw_ref[...] * p1) * scale
    cos, sin = sincos(m_row_ref[...] * float(middle), turn)
    real = lax.broadcasted_iota(jnp.int32, (1, LANES), 1) % 4 < 2
    other = jnp.where(real, pltpu.roll(leg, LANES - 2, 1), pltpu.roll(leg, 2, 1))
    leg = (leg * cos + other * jnp.where(real, -sin, sin)).astype(BF16)
    src = lax.broadcasted_iota(jnp.int32, (rows, rows), 0)
    dst = lax.broadcasted_iota(jnp.int32, (rows, rows), 1)
    slots = rows // 4
    order = jnp.where((src % 4) * slots + src // 4 == dst, 1.0, 0.0).astype(BF16)
    out_ref[...] = jnp.dot(leg, order, preferred_element_type=F32).astype(BF16)


def legendre(x, own_ids, lat_rows, period, middle, turn, scale):
    rows, waves = x.shape
    lats = lat_rows.shape[0]
    ids = jnp.repeat(own_ids, 4)
    return pl.pallas_call(
        functools.partial(legendre_kernel, period, middle, turn, scale),
        out_shape=jax.ShapeDtypeStruct((lats, rows), BF16),
        scratch_shapes=[
            pltpu.VMEM((lats, waves), BF16),
            pltpu.VMEM((lats, waves), BF16),
            pltpu.VMEM((lats, LANES), F32),
            pltpu.VMEM((lats, LANES), F32),
        ],
        compiler_params=pltpu.CompilerParams(vmem_limit_bytes=24 << 20),
        name="legendre",
    )(x, ids[:, None], ids[None, :].astype(F32), lat_rows.astype(F32)[:, None])


def times_i(z, power):
    re, im = z
    return ((re, im), (-im, re), (-re, -im), (im, -re))[power % 4]


def add(*terms):
    re, im = terms[0]
    for r, i in terms[1:]:
        re, im = re + r, im + i
    return re, im


def four(z):
    a, b = add(z[0], z[2]), add(z[0], times_i(z[2], 2))
    c, d = add(z[1], z[3]), add(z[1], times_i(z[3], 2))
    return add(a, c), add(b, times_i(d, 1)), add(a, times_i(c, 2)), add(b, times_i(d, 3))


def sixteen_real(y):
    inner = [four([y[4 * q1 + q0] for q1 in range(4)]) for q0 in range(4)]
    out = [None] * 16
    for a0 in range(4):
        v = []
        for q0 in range(4):
            re, im = inner[q0][a0]
            if q0 * a0:
                angle = 2.0 * math.pi * q0 * a0 / 16.0
                cos, sin = math.cos(angle), math.sin(angle)
                re, im = re * cos - im * sin, re * sin + im * cos
            v.append((re, im))
        even, odd = v[0][0] + v[2][0], v[0][0] - v[2][0]
        plus, minus = v[1][0] + v[3][0], v[3][1] - v[1][1]
        out[a0], out[a0 + 8] = even + plus, even - plus
        out[a0 + 4], out[a0 + 12] = odd + minus, odd - minus
    return out


def table_kernel(period, m_ref, e_ref):
    waves = m_ref.shape[1]
    spans = e_ref.shape[0] // LANES
    odd = 2.0 * lax.broadcasted_iota(jnp.int32, (8, LANES), 0).astype(F32) + 1.0

    def fill(i, carry):
        at = pl.ds(pl.multiple_of(i * LANES, LANES), LANES)
        m = jnp.broadcast_to(m_ref[:, at], (8, LANES))
        c8, s8 = sincos(m * 16.0, period)
        c64, s64 = sincos(m * 128.0, period)
        z = [sincos(m * odd, period)]
        for _ in range(7):
            z.append(rotate(*z[-1], c8, s8))
        for t in range(spans):
            base = 256 * (t // 2) + 64 * (t % 2)
            for h in range(4):
                (c0, s0), (c1, s1) = z[2 * h], z[2 * h + 1]
                e_ref[pl.ds(base + h * 16, 16), at] = jnp.concatenate([c0, c1], axis=0).astype(BF16)
                e_ref[pl.ds(base + 128 + h * 16, 16), at] = jnp.concatenate([s0, s1], axis=0).astype(BF16)
            if t + 1 < spans:
                z = [rotate(a, b, c64, s64) for a, b in z]
        return carry

    lax.fori_loop(0, waves // LANES, fill, 0)


def fourier_table(m, period, tiles):
    waves = m.shape[1]
    return pl.pallas_call(
        functools.partial(table_kernel, period),
        out_shape=jax.ShapeDtypeStruct((tiles * LANES, waves), BF16),
        in_specs=[pl.BlockSpec(memory_space=pltpu.VMEM)],
        out_specs=pl.BlockSpec(memory_space=pltpu.VMEM),
        compiler_params=pltpu.CompilerParams(vmem_limit_bytes=8 << 20),
        cost_estimate=pl.CostEstimate(flops=20000000, bytes_accessed=2500000, transcendentals=0),
        name="fourier_table",
    )(m)


def fourier_kernel(scale, z_ref, m_ref, stamp_ref, e_ref, out_ref, l_ref, d_ref, g_ref):
    waves = m_ref.shape[1]
    group = lax.broadcasted_iota(jnp.int32, (8, LANES), 1) // 32

    def spread(i, carry):
        at = pl.ds(pl.multiple_of(i * LANES, LANES), LANES)
        block = [z_ref[4 * i + u].astype(F32) for u in range(4)]
        parts = []
        for cf in range(4):
            whole = None
            for u in range(4):
                turn = (32 * (u - cf)) % LANES
                moved = pltpu.roll(block[u], turn, 1) if turn else block[u]
                whole = moved if whole is None else jnp.where(group == u, moved, whole)
            parts.append(whole)
        both = jnp.concatenate(parts, axis=0)
        m = jnp.broadcast_to(m_ref[:, at], both.shape)
        residue = m - 16.0 * jnp.floor(m * 0.0625)
        for q in range(16):
            l_ref[pl.ds(q * 32, 32), at] = jnp.where(residue == float(q), both, 0.0).astype(BF16)
        return carry

    lax.fori_loop(0, waves // LANES, spread, 0)
    halves = e_ref.shape[0] // 256
    low, high = pl.ds(0, LANES), pl.ds(LANES, LANES)
    for p in range(halves):
        d_ref[...] = lax.dot_general(l_ref[...], e_ref[pl.ds(p * 256, 256), :], NT, preferred_element_type=F32)
        right, left = [], []
        for q in range(16):
            re, im = pl.ds(q * 32, 16), pl.ds(q * 32 + 16, 16)
            c0, c1, s0, s1 = d_ref[re, low], d_ref[im, low], d_ref[re, high], d_ref[im, high]
            right.append((c0 - s1, c1 + s0))
            left.append((c0 + s1, c1 - s0))
        for side, y in ((halves + p, right), (halves - 1 - p, left)):
            for a, value in enumerate(sixteen_real(y)):
                g_ref[side, pl.ds(a * 16, 16), :] = (value * scale).astype(BF16)

    src = lax.broadcasted_iota(jnp.int32, (LANES, LANES), 0)
    dst = lax.broadcasted_iota(jnp.int32, (LANES, LANES), 1)
    half = LANES // 2

    def pick(mirrored, upper):
        want = (half - 1 + LANES * upper - dst) if mirrored else (dst + half - LANES * upper)
        inside = (dst >= half) if upper else (dst < half)
        return jnp.where(inside & (src == want), 1.0, 0.0).astype(BF16)

    lane = lax.broadcasted_iota(jnp.int32, (16, LANES), 1)
    unused = (lane >= STAMP_LANE) & (lane < LANES - STAMP_LANE)
    stamp = jnp.broadcast_to(stamp_ref[...], (16, LANES))
    tiles = 2 * halves
    for t in range(tiles):
        first, second = t, (t + 1) % tiles
        value = jnp.dot(g_ref[first], pick(first < halves, 0), preferred_element_type=F32) + jnp.dot(
            g_ref[second], pick(second < halves, 1), preferred_element_type=F32
        )
        for a in range(16):
            got = value[a * 16 : (a + 1) * 16]
            if t == tiles - 1:
                got = jnp.where(unused, stamp, got)
            out_ref[a, pl.ds(t * 16, 16), :] = got.astype(BF16)


def fourier(z, m, stamp, table, scale):
    tiles = table.shape[0] // LANES
    vmem = pl.BlockSpec(memory_space=pltpu.VMEM)
    return pl.pallas_call(
        functools.partial(fourier_kernel, scale),
        out_shape=jax.ShapeDtypeStruct((16, tiles * 16, LANES), BF16),
        in_specs=[vmem] * 4,
        out_specs=vmem,
        scratch_shapes=[
            pltpu.VMEM((512, table.shape[1]), BF16),
            pltpu.VMEM((512, 256), F32),
            pltpu.VMEM((tiles, 256, LANES), BF16),
        ],
        compiler_params=pltpu.CompilerParams(vmem_limit_bytes=24 << 20),
        name="fourier",
    )(z, m, stamp, table)


def put_row(row, rows, at, value, out_ref, last_ref, first_ref):
    out_ref[(row, *at)] = value
    if row >= rows - ABOVE:
        last_ref[(row - rows + ABOVE, *at)] = value
    if row < BELOW:
        first_ref[(row, *at)] = value


def state_shapes(rows, tiles, fields):
    return [jax.ShapeDtypeStruct((n, tiles, fields, LANES), BF16) for n in (rows, ABOVE, BELOW)]


def regroup_kernel(x_ref, out_ref, last_ref, first_ref, wide_ref):
    rows, tiles = out_ref.shape[:2]
    sources = x_ref.shape[0]
    span = x_ref.shape[1]
    for v in range(sources):
        wide_ref[pl.ds(v * span, span), :] = x_ref[v].astype(F32)
    for j in range(rows):
        for t in range(tiles):
            for f in range(2):
                got = wide_ref[pl.ds(t * 16 + f * 8 + j, sources, stride=span), :]
                put_row(j, rows, (t, pl.ds(f * sources, sources)), got.astype(BF16), out_ref, last_ref, first_ref)


def regroup(x):
    return pl.pallas_call(
        regroup_kernel,
        out_shape=state_shapes(8, x.shape[1] // 16, 32),
        scratch_shapes=[pltpu.VMEM((x.shape[0] * x.shape[1], LANES), F32)],
        compiler_params=pltpu.CompilerParams(vmem_limit_bytes=8 << 20),
        name="regroup",
    )(x)


def advance_kernel(last, move_ref, weight_ref, before_ref, now_ref, after_ref, phys_ref, bias_ref, *refs):
    rows, tiles, fields = now_ref.shape[:3]
    s_ref = refs[-1]
    s_ref[pl.ds(0, ABOVE)] = before_ref[...]
    s_ref[pl.ds(ABOVE, rows)] = now_ref[...]
    s_ref[pl.ds(ABOVE + rows, BELOW)] = after_ref[...]
    lane = lax.broadcasted_iota(jnp.int32, (fields, LANES), 1)
    left_half = lane < LANES // 2
    phys = phys_ref[...]
    bias = jnp.broadcast_to(bias_ref[...], (fields, LANES))

    def departed(band, block, tile):
        where = band * 7 + block
        base = ABOVE - 2 + band * BLOCK_ROWS - move_ref[2 * where]
        first = -move_ref[2 * where + 1] - 2
        wr = [weight_ref[8 * where + a] for a in range(4)]
        wc = [weight_ref[8 * where + 4 + a] for a in range(4)]
        centre, edge = [], []
        for k in range(BLOCK_ROWS + 3):
            before = s_ref[base + k, (tile + tiles - 1) % tiles].astype(F32)
            after = s_ref[base + k, (tile + 1) % tiles].astype(F32)
            centre.append(s_ref[base + k, tile].astype(F32))
            edge.append(jnp.where(left_half, after, before))
        taps = []
        for b in range(4):
            shift = first + b
            outside = (lane < shift) | (lane >= LANES + shift)
            taps.append((outside, (LANES - shift) & (LANES - 1)))
        result = []
        for i in range(BLOCK_ROWS):
            c = sum(wr[a] * centre[i + a] for a in range(4))
            e = sum(wr[a] * edge[i + a] for a in range(4))
            total = None
            for b in range(4):
                outside, turn = taps[b]
                term = wc[b] * pltpu.roll(jnp.where(outside, e, c), turn, 1)
                total = term if total is None else total + term
            result.append(total)
        return result

    for band in range(rows // BLOCK_ROWS):
        for tile in range(5 if last else 6):
            if tile < 5:
                dep = departed(band, tile + 1, tile)
            else:
                right = departed(band, 6, tile)
                left = departed(band, 0, tile)
                dep = [jnp.where(left_half, r, l) for r, l in zip(right, left)]
            low = jnp.concatenate(dep, axis=1).astype(BF16)
            forcing = jnp.dot(phys, low, preferred_element_type=F32)
            for i in range(BLOCK_ROWS):
                push = forcing[:, i * LANES : (i + 1) * LANES] + bias
                value = dep[i] + jnp.tanh(push)
                row = band * BLOCK_ROWS + i
                if last:
                    refs[1][pl.ds((row * 5 + tile) * fields, fields), :] = value
                else:
                    put_row(row, rows, (tile,), value.astype(BF16), *refs[:3])
    if last:
        for f in range(fields):
            kept = (f % 2) * (fields // 2) + f // 2
            for t in range(5):
                got = refs[1][pl.ds(t * fields + kept, rows, stride=5 * fields), :]
                refs[0][f, :, pl.ds(t * LANES, LANES)] = got.astype(BF16)


def advance(last, moves, weights, before, now, after, phys, bias):
    rows, tiles, fields = now.shape[:3]
    smem, vmem = pl.BlockSpec(memory_space=pltpu.SMEM), pl.BlockSpec(memory_space=pltpu.VMEM)
    scratch = [pltpu.VMEM((ABOVE + rows + BELOW, tiles, fields, LANES), BF16)]
    if last:
        shape = jax.ShapeDtypeStruct((fields, rows, 5 * LANES), BF16)
        scratch.insert(0, pltpu.VMEM((rows * 5 * fields, LANES), F32))
    else:
        shape = state_shapes(rows, tiles, fields)
    return pl.pallas_call(
        functools.partial(advance_kernel, last),
        out_shape=shape,
        in_specs=[smem, smem] + [vmem] * 5,
        scratch_shapes=scratch,
        compiler_params=pltpu.CompilerParams(vmem_limit_bytes=16 << 20),
        name="advance_last" if last else "advance_first",
    )(moves, weights, before, now, after, phys, bias)


def cubic_weights(fraction):
    coord = 1.0 - fraction
    return (
        -coord * (coord - 1.0) * (coord - 2.0) / 6.0,
        (coord + 1.0) * (coord - 1.0) * (coord - 2.0) / 2.0,
        -(coord + 1.0) * coord * (coord - 2.0) / 2.0,
        (coord + 1.0) * coord * (coord - 1.0) / 6.0,
    )


def three_parts(value):
    high = lax.reduce_precision(value, 8, 7)
    mid = lax.reduce_precision(value - high, 8, 7)
    return high, mid, value - high - mid


def edge_stamp(shift_rows, shift_cols, frac_rows, frac_cols):
    pieces = [shift_rows.astype(F32), shift_cols.astype(F32), *three_parts(frac_rows), *three_parts(frac_cols)]
    table = jnp.stack(pieces, axis=0)
    edges = jnp.concatenate([table[:, :, :1], table[:, :, -1:]], axis=2)
    flat = edges.reshape(1, -1)
    return jnp.pad(flat, ((0, 0), (STAMP_LANE, LANES - STAMP_LANE - flat.shape[1])))


def read_stamp(lanes, side):
    table = lanes.astype(F32).reshape(8, 2, 2)[:, :, side : side + 1]
    return table[0], table[1], table[2] + table[3] + table[4], table[5] + table[6] + table[7]


def block_tables(shift_rows, shift_cols, frac_rows, frac_cols):
    moves = jnp.stack([shift_rows, shift_cols], axis=-1).astype(jnp.int32).reshape(-1)
    weights = jnp.stack(cubic_weights(frac_rows) + cubic_weights(frac_cols), axis=-1).reshape(-1)
    return moves, weights


def row_halos(last, first):
    size = lax.axis_size("wave")
    before = lax.ppermute(last, "wave", [(i, i + 1) for i in range(size - 1)])
    after = lax.ppermute(first, "wave", [(i + 1, i) for i in range(size - 1)])
    return before, after


def shards(spectral, wave_ids, lat_rows, shift_rows, shift_cols, frac_rows, frac_cols, phys_weight, phys_bias):
    slots, parts, fields, waves = spectral.shape
    lats = lat_rows.shape[0]
    bands, owners = lax.axis_size("wave"), lax.axis_size("lev")
    nlon = shift_rows.shape[2] * BLOCK_COLS * owners
    scale = 1.0 / math.sqrt(waves)
    own_ids = lax.dynamic_slice_in_dim(wave_ids, lax.axis_index("wave") * slots, slots)
    outgoing = legendre(spectral.reshape(slots * parts * fields, waves), own_ids, lat_rows, 8 * lats, nlon // owners - 1, 2 * nlon, scale)
    outgoing = outgoing.reshape(bands, lats // bands, slots * parts * fields)
    arrived = lax.all_to_all(outgoing, "wave", split_axis=0, concat_axis=0, tiled=True)
    m = wave_ids.astype(F32)[None, :]
    table = fourier_table(m, 2 * nlon, 6)
    stamp = edge_stamp(shift_rows[0], shift_cols[0], frac_rows[0], frac_cols[0])
    own = (shift_rows.astype(F32), shift_cols.astype(F32), frac_rows, frac_cols)
    second = block_tables(*[jnp.pad(o[1], ((0, 0), (1, 1))) for o in own])
    split = (owners, fields)
    phys = phys_weight.reshape(split + split).transpose(1, 0, 3, 2).reshape(phys_weight.shape)
    bias = phys_bias.reshape(split).T.reshape(-1, 1)
    arrived, second, phys, bias = lax.optimization_barrier((arrived, second, phys, bias))
    columns = fourier(arrived, m, stamp, table, scale)
    columns = lax.all_to_all(columns, "lev", split_axis=0, concat_axis=0, tiled=True)
    state, *edges = regroup(columns)
    before, after = row_halos(*edges)

    me = lax.axis_index("lev")
    stamp_row = columns.shape[1] - 16
    size = (1, 1, 32)
    west = lax.dynamic_slice(columns, ((me + owners - 1) % owners, stamp_row, STAMP_LANE), size)
    east = lax.dynamic_slice(columns, ((me + 1) % owners, stamp_row, STAMP_LANE), size)
    west, east = read_stamp(west, 1), read_stamp(east, 0)
    first = [jnp.concatenate([w, o[0], e], axis=1) for w, o, e in zip(west, own, east)]
    state, *edges = advance(False, *block_tables(*first), before, state, after, phys, bias)
    before, after = row_halos(*edges)
    return advance(True, *second, before, state, after, phys, bias)


def solution(mesh):
    blocks = P(None, "wave", "lev")
    return jax.shard_map(
        shards,
        mesh=mesh,
        in_specs=(P("wave", None, "lev", None), P(), P(), blocks, blocks, blocks, blocks, P(), P()),
        out_specs=P(None, "wave", "lev"),
        check_vma=False,
    )
```

```python
import functools
import math

import jax
import jax.numpy as jnp
from jax import lax
from jax.experimental import pallas as pl
from jax.experimental.pallas import tpu as pltpu
from jax.sharding import PartitionSpec as P

BLOCK_ROWS = 4
BLOCK_COLS = 128
LANES = 128
ABOVE = 6
BELOW = 5
HALO = 16
STAMP_LANE = 4 * HALO
PER_BLOCK = 10
F32 = jnp.float32
BF16 = jnp.bfloat16
NT = (((1,), (1,)), ((), ()))


def sincos(x, period):
    quarter = period // 4
    turns = jnp.floor(x * (1.0 / quarter) + 0.5)
    t = (x - turns * float(quarter)) * (2.0 * math.pi / period)
    t2 = t * t
    s = t * (1.0 + t2 * (-1.0 / 6.0 + t2 * (1.0 / 120.0 + t2 * (-1.0 / 5040.0))))
    c = 1.0 + t2 * (-0.5 + t2 * (1.0 / 24.0 + t2 * (-1.0 / 720.0 + t2 * (1.0 / 40320.0))))
    k = turns.astype(jnp.int32)
    swap = (k & 1) == 1
    cos, sin = jnp.where(swap, s, c), jnp.where(swap, c, s)
    cos = jnp.where(((k + 1) & 2) != 0, -cos, cos)
    sin = jnp.where((k & 2) != 0, -sin, sin)
    return cos, sin


def rotate(c, s, rc, rs):
    return c * rc - s * rs, s * rc + c * rs


def down(row):
    return jnp.broadcast_to(row, (LANES, LANES)).T


def legendre_kernel(
    period, middle, turn, scale, ids_ref, lat_in_ref, band_ref, x_ref, out_ref, cos_ref, sin_ref, cw_ref, sw_ref, lat_ref
):
    rows, waves = x_ref.shape
    lats = out_ref.shape[0]
    slots = rows // 4
    step = 32
    lane = lax.broadcasted_iota(jnp.int32, (1, LANES), 1)
    first = band_ref[0] * slots
    m_row = jnp.zeros((1, LANES), jnp.int32)
    for s in range(slots):
        m_row = jnp.where(lane // 4 == s, ids_ref[first + s], m_row)
    m_col = down(m_row.astype(F32))
    m_row = m_row.astype(F32)
    for i in range(lats // LANES):
        lat_ref[pl.ds(i * LANES, LANES), :] = down(lat_in_ref[:, pl.ds(i * LANES, LANES)].astype(F32))
    wide_lane = lax.broadcasted_iota(jnp.int32, (step, LANES), 1).astype(F32)
    wide_m = jnp.broadcast_to(m_row, (step, LANES))

    def fill(i, carry):
        at = pl.ds(pl.multiple_of(i * step, step), step)
        lat = lat_ref[at, :]
        cw, sw = sincos(lat * wide_m, period)
        cw_ref[at, :] = cw
        sw_ref[at, :] = sw
        c, s = sincos(lat * wide_lane, period)
        rc, rs = sincos(lat * float(LANES), period)
        for a in range(waves // LANES):
            cols = pl.ds(a * LANES, LANES)
            cos_ref[at, cols] = c.astype(BF16)
            sin_ref[at, cols] = s.astype(BF16)
            if a + 1 < waves // LANES:
                c, s = rotate(c, s, rc, rs)
        return carry

    lax.fori_loop(0, lats // step, fill, 0)
    kept = []
    k = lax.broadcasted_iota(jnp.int32, (rows, LANES), 1).astype(F32)
    for a in range(waves // LANES):
        part = x_ref[:, pl.ds(a * LANES, LANES)].astype(F32)
        kept.append(jnp.where(k < (waves - a * LANES) - m_col, part, 0.0).astype(BF16))
    x = jnp.concatenate(kept, axis=1)
    p0 = lax.dot_general(cos_ref[...], x, NT, preferred_element_type=F32)
    p1 = lax.dot_general(sin_ref[...], x, NT, preferred_element_type=F32)
    leg = (cw_ref[...] * p0 - sw_ref[...] * p1) * scale
    cos, sin = sincos(m_row * float(middle), turn)
    real = lane % 4 < 2
    other = jnp.where(real, pltpu.roll(leg, LANES - 2, 1), pltpu.roll(leg, 2, 1))
    leg = (leg * cos + other * jnp.where(real, -sin, sin)).astype(BF16)
    src = lax.broadcasted_iota(jnp.int32, (rows, rows), 0)
    dst = lax.broadcasted_iota(jnp.int32, (rows, rows), 1)
    order = jnp.where((src % 4) * slots + src // 4 == dst, 1.0, 0.0).astype(BF16)
    out_ref[...] = jnp.dot(leg, order, preferred_element_type=F32).astype(BF16)


def legendre(x, wave_ids, band, lat_rows, period, middle, turn, scale):
    rows, waves = x.shape
    lats = lat_rows.shape[0]
    smem, vmem = pl.BlockSpec(memory_space=pltpu.SMEM), pl.BlockSpec(memory_space=pltpu.VMEM)
    return pl.pallas_call(
        functools.partial(legendre_kernel, period, middle, turn, scale),
        out_shape=jax.ShapeDtypeStruct((lats, rows), BF16),
        in_specs=[smem, vmem, smem, vmem],
        out_specs=vmem,
        scratch_shapes=[
            pltpu.VMEM((lats, waves), BF16),
            pltpu.VMEM((lats, waves), BF16),
            pltpu.VMEM((lats, LANES), F32),
            pltpu.VMEM((lats, LANES), F32),
            pltpu.VMEM((lats, LANES), F32),
        ],
        compiler_params=pltpu.CompilerParams(vmem_limit_bytes=24 << 20),
        name="legendre",
    )(wave_ids, lat_rows.reshape(1, -1), band, x)


def times_i(z, power):
    re, im = z
    return ((re, im), (-im, re), (-re, -im), (im, -re))[power % 4]


def add(*terms):
    re, im = terms[0]
    for r, i in terms[1:]:
        re, im = re + r, im + i
    return re, im


def four(z):
    a, b = add(z[0], z[2]), add(z[0], times_i(z[2], 2))
    c, d = add(z[1], z[3]), add(z[1], times_i(z[3], 2))
    return add(a, c), add(b, times_i(d, 1)), add(a, times_i(c, 2)), add(b, times_i(d, 3))


def sixteen_real(y):
    inner = [four([y[4 * q1 + q0] for q1 in range(4)]) for q0 in range(4)]
    out = [None] * 16
    for a0 in range(4):
        v = []
        for q0 in range(4):
            re, im = inner[q0][a0]
            if q0 * a0:
                angle = 2.0 * math.pi * q0 * a0 / 16.0
                cos, sin = math.cos(angle), math.sin(angle)
                re, im = re * cos - im * sin, re * sin + im * cos
            v.append((re, im))
        even, odd = v[0][0] + v[2][0], v[0][0] - v[2][0]
        plus, minus = v[1][0] + v[3][0], v[3][1] - v[1][1]
        out[a0], out[a0 + 8] = even + plus, even - plus
        out[a0 + 4], out[a0 + 12] = odd + minus, odd - minus
    return out


def cubic_weights(fraction):
    coord = 1.0 - fraction
    return (
        -coord * (coord - 1.0) * (coord - 2.0) * (1.0 / 6.0),
        (coord + 1.0) * (coord - 1.0) * (coord - 2.0) * 0.5,
        -(coord + 1.0) * coord * (coord - 2.0) * 0.5,
        (coord + 1.0) * coord * (coord - 1.0) * (1.0 / 6.0),
    )


def table_kernel(period, ids_ref, sr_ref, sc_ref, fr_ref, fc_ref, e_ref, m_ref, stamp_ref, param_ref):
    waves = ids_ref.shape[1]
    spans = e_ref.shape[0] // LANES
    odd = 2.0 * lax.broadcasted_iota(jnp.int32, (8, LANES), 0).astype(F32) + 1.0
    m_ref[...] = ids_ref[...].astype(F32)

    def fill(i, carry):
        at = pl.ds(pl.multiple_of(i * LANES, LANES), LANES)
        m = jnp.broadcast_to(ids_ref[:, at].astype(F32), (8, LANES))
        c8, s8 = sincos(m * 16.0, period)
        c64, s64 = sincos(m * 128.0, period)
        z = [sincos(m * odd, period)]
        for _ in range(7):
            z.append(rotate(*z[-1], c8, s8))
        for t in range(spans):
            base = 256 * (t // 2) + 64 * (t % 2)
            for h in range(4):
                (c0, s0), (c1, s1) = z[2 * h], z[2 * h + 1]
                e_ref[pl.ds(base + h * 16, 16), at] = jnp.concatenate([c0, c1], axis=0).astype(BF16)
                e_ref[pl.ds(base + 128 + h * 16, 16), at] = jnp.concatenate([s0, s1], axis=0).astype(BF16)
            if t + 1 < spans:
                z = [rotate(a, b, c64, s64) for a, b in z]
        return carry

    lax.fori_loop(0, waves // LANES, fill, 0)
    steps, bands, blocks = sr_ref.shape
    lane = lax.broadcasted_iota(jnp.int32, (8, LANES), 1)
    row = lax.broadcasted_iota(jnp.int32, (8, LANES), 0)
    stamp = jnp.zeros((8, LANES), F32)
    for step in range(steps):
        for band in range(bands):
            for block in range(blocks):
                moves = (sr_ref[step, band, block].astype(F32), sc_ref[step, band, block].astype(F32))
                values = moves + cubic_weights(fr_ref[step, band, block]) + cubic_weights(fc_ref[step, band, block])
                for k, value in enumerate(values):
                    param_ref[((step * bands + band) * blocks + block) * PER_BLOCK + k] = value
                    side = {0: 0, blocks - 1: 1}.get(block)
                    if step == 0 and side is not None:
                        at = STAMP_LANE + (side * bands + band) * PER_BLOCK + k
                        stamp = jnp.where(lane == at, value, stamp)
    high = stamp.astype(BF16).astype(F32)
    mid = (stamp - high).astype(BF16).astype(F32)
    stamp_ref[...] = jnp.where(row == 0, high, jnp.where(row == 1, mid, jnp.where(row == 2, stamp - high - mid, 0.0)))


def fourier_table(ids, shift_rows, shift_cols, frac_rows, frac_cols, period, tiles):
    waves = ids.shape[1]
    smem, vmem = pl.BlockSpec(memory_space=pltpu.SMEM), pl.BlockSpec(memory_space=pltpu.VMEM)
    return pl.pallas_call(
        functools.partial(table_kernel, period),
        out_shape=[
            jax.ShapeDtypeStruct((tiles * LANES, waves), BF16),
            jax.ShapeDtypeStruct((1, waves), F32),
            jax.ShapeDtypeStruct((8, LANES), F32),
            jax.ShapeDtypeStruct((shift_rows.size * PER_BLOCK,), F32),
        ],
        in_specs=[vmem] + [smem] * 4,
        out_specs=[vmem, vmem, vmem, smem],
        compiler_params=pltpu.CompilerParams(vmem_limit_bytes=8 << 20),
        cost_estimate=pl.CostEstimate(flops=20000000, bytes_accessed=2500000, transcendentals=0),
        name="fourier_table",
    )(ids, shift_rows, shift_cols, frac_rows, frac_cols)


def fourier_kernel(scale, z_ref, m_ref, stamp_ref, e_ref, out_ref, l_ref, d_ref, g_ref):
    waves = m_ref.shape[1]
    group = lax.broadcasted_iota(jnp.int32, (8, LANES), 1) // 32

    def spread(i, carry):
        at = pl.ds(pl.multiple_of(i * LANES, LANES), LANES)
        block = [z_ref[4 * i + u].astype(F32) for u in range(4)]
        parts = []
        for cf in range(4):
            whole = None
            for u in range(4):
                turn = (32 * (u - cf)) % LANES
                moved = pltpu.roll(block[u], turn, 1) if turn else block[u]
                whole = moved if whole is None else jnp.where(group == u, moved, whole)
            parts.append(whole)
        both = jnp.concatenate(parts, axis=0)
        m = jnp.broadcast_to(m_ref[:, at], both.shape)
        residue = m - 16.0 * jnp.floor(m * 0.0625)
        for q in range(16):
            l_ref[pl.ds(q * 32, 32), at] = jnp.where(residue == float(q), both, 0.0).astype(BF16)
        return carry

    lax.fori_loop(0, waves // LANES, spread, 0)
    halves = e_ref.shape[0] // 256
    low, high = pl.ds(0, LANES), pl.ds(LANES, LANES)
    for p in range(halves):
        d_ref[...] = lax.dot_general(l_ref[...], e_ref[pl.ds(p * 256, 256), :], NT, preferred_element_type=F32)
        right, left = [], []
        for q in range(16):
            re, im = pl.ds(q * 32, 16), pl.ds(q * 32 + 16, 16)
            c0, c1, s0, s1 = d_ref[re, low], d_ref[im, low], d_ref[re, high], d_ref[im, high]
            right.append((c0 - s1, c1 + s0))
            left.append((c0 + s1, c1 - s0))
        for side, y in ((halves + p, right), (halves - 1 - p, left)):
            for a, value in enumerate(sixteen_real(y)):
                g_ref[side, pl.ds(a * 16, 16), :] = (value * scale).astype(BF16)

    src = lax.broadcasted_iota(jnp.int32, (LANES, LANES), 0)
    dst = lax.broadcasted_iota(jnp.int32, (LANES, LANES), 1)
    half = LANES // 2

    def pick(mirrored, upper):
        want = (half - 1 + LANES * upper - dst) if mirrored else (dst + half - LANES * upper)
        inside = (dst >= half) if upper else (dst < half)
        return jnp.where(inside & (src == want), 1.0, 0.0).astype(BF16)

    lane = lax.broadcasted_iota(jnp.int32, (8, LANES), 1)
    stamp = stamp_ref[...]
    tiles = 2 * halves
    for t in range(tiles):
        first, second = t, (t + 1) % tiles
        value = jnp.dot(g_ref[first], pick(first < halves, 0), preferred_element_type=F32) + jnp.dot(
            g_ref[second], pick(second < halves, 1), preferred_element_type=F32
        )
        for a in range(16):
            one, two = value[a * 16 : a * 16 + 8], value[a * 16 + 8 : a * 16 + 16]
            if t < tiles - 1:
                out_ref[a, pl.ds(t * 8, 8), :] = one.astype(BF16)
                out_ref[a, pl.ds((tiles - 1 + t) * 8, 8), :] = two.astype(BF16)
            else:
                one, two = pltpu.roll(one, HALO, 1), pltpu.roll(two, 3 * HALO, 1)
                halo = jnp.where(lane < 2 * HALO, one, jnp.where(lane < STAMP_LANE, two, stamp))
                out_ref[a, pl.ds((tiles - 1) * 16, 8), :] = halo.astype(BF16)


def fourier(z, m, stamp, table, scale):
    tiles = table.shape[0] // LANES
    vmem = pl.BlockSpec(memory_space=pltpu.VMEM)
    return pl.pallas_call(
        functools.partial(fourier_kernel, scale),
        out_shape=jax.ShapeDtypeStruct((16, tiles * 16 - 8, LANES), BF16),
        in_specs=[vmem] * 4,
        out_specs=vmem,
        scratch_shapes=[
            pltpu.VMEM((512, table.shape[1]), BF16),
            pltpu.VMEM((512, 256), F32),
            pltpu.VMEM((tiles, 256, LANES), BF16),
        ],
        compiler_params=pltpu.CompilerParams(vmem_limit_bytes=24 << 20),
        name="fourier",
    )(z, m, stamp, table)


def put_row(row, rows, at, value, out_ref, last_ref, first_ref):
    out_ref[(row, *at)] = value
    if row >= rows - ABOVE:
        last_ref[(row - rows + ABOVE, *at)] = value
    if row < BELOW:
        first_ref[(row, *at)] = value


def state_shapes(rows, tiles, fields):
    return [jax.ShapeDtypeStruct((n, tiles, fields, LANES), BF16) for n in (rows, ABOVE, BELOW)]


def regroup_kernel(owner_ref, x_ref, out_ref, last_ref, first_ref, edge_ref, wide_ref):
    rows, tiles, fields = out_ref.shape[:3]
    sources = x_ref.shape[0]
    main, span = (tiles - 1) * rows, tiles * rows
    for v in range(sources):
        halo = x_ref[v, pl.ds(2 * main, rows), :].astype(F32)
        for f in range(2):
            at = (2 * v + f) * span
            wide_ref[pl.ds(at, main), :] = x_ref[v, pl.ds(f * main, main), :].astype(F32)
            wide_ref[pl.ds(at + main, rows), :] = pltpu.roll(halo, LANES - HALO - 2 * HALO * f, 1)
    for j in range(rows):
        for t in range(tiles):
            got = wide_ref[pl.ds(t * rows + j, fields, stride=span), :]
            put_row(j, rows, (t,), got.astype(BF16), out_ref, last_ref, first_ref)
    owner = owner_ref[0]
    edges = []
    for source in ((owner + sources - 1) % sources, (owner + 1) % sources):
        parts = x_ref[source, pl.ds(2 * main, rows), :].astype(F32)
        edges.append(parts[0:1] + parts[1:2] + parts[2:3])
    edge_ref[...] = jnp.concatenate(edges, axis=0)


def regroup(x, owner):
    smem, vmem = pl.BlockSpec(memory_space=pltpu.SMEM), pl.BlockSpec(memory_space=pltpu.VMEM)
    tiles = (x.shape[1] + 8) // 16
    return pl.pallas_call(
        regroup_kernel,
        out_shape=state_shapes(8, tiles, 32) + [jax.ShapeDtypeStruct((2, LANES), F32)],
        in_specs=[smem, vmem],
        out_specs=[vmem] * 4,
        scratch_shapes=[pltpu.VMEM((32 * tiles * 8, LANES), F32)],
        compiler_params=pltpu.CompilerParams(vmem_limit_bytes=8 << 20),
        name="regroup",
    )(owner, x)


def advance_kernel(last, param_ref, edge_ref, before_ref, now_ref, after_ref, phys_ref, bias_ref, *refs):
    rows, tiles, fields = now_ref.shape[:3]
    s_ref = refs[-1]
    s_ref[pl.ds(0, ABOVE)] = before_ref[...]
    s_ref[pl.ds(ABOVE, rows)] = now_ref[...]
    s_ref[pl.ds(ABOVE + rows, BELOW)] = after_ref[...]
    bands = rows // BLOCK_ROWS
    lane = lax.broadcasted_iota(jnp.int32, (fields, LANES), 1)
    left_half = lane < LANES // 2
    phys = phys_ref[...]
    bias = jnp.broadcast_to(bias_ref[...], (LANES, fields)).T

    def departed(band, block, tile):
        if 0 <= block < 5:
            start = ((last * bands + band) * 5 + block) * PER_BLOCK
            value = [param_ref[start + k] for k in range(PER_BLOCK)]
        else:
            west = block < 0
            start = STAMP_LANE + (west * bands + band) * PER_BLOCK
            value = [edge_ref[0 if west else 1, start + k] for k in range(PER_BLOCK)]
        base = ABOVE - 2 + band * BLOCK_ROWS - value[0].astype(jnp.int32)
        first = -value[1].astype(jnp.int32) - 2
        wr, wc = value[2:6], value[6:10]
        centre, edge = [], []
        for k in range(BLOCK_ROWS + 3):
            before = s_ref[base + k, (tile + tiles - 1) % tiles].astype(F32)
            after = s_ref[base + k, (tile + 1) % tiles].astype(F32)
            centre.append(s_ref[base + k, tile].astype(F32))
            edge.append(jnp.where(left_half, after, before))
        taps = []
        for b in range(4):
            shift = first + b
            outside = (lane < shift) | (lane >= LANES + shift)
            taps.append((outside, (LANES - shift) & (LANES - 1)))
        result = []
        for i in range(BLOCK_ROWS):
            c = sum(wr[a] * centre[i + a] for a in range(4))
            e = sum(wr[a] * edge[i + a] for a in range(4))
            total = None
            for b in range(4):
                outside, turn = taps[b]
                term = wc[b] * pltpu.roll(jnp.where(outside, e, c), turn, 1)
                total = term if total is None else total + term
            result.append(total)
        return result

    for band in range(bands):
        for tile in range(5 if last else 6):
            if tile < 5:
                dep = departed(band, tile, tile)
            else:
                right = departed(band, 5, tile)
                left = departed(band, -1, tile)
                dep = [jnp.where(left_half, r, l) for r, l in zip(right, left)]
            low = jnp.concatenate(dep, axis=1).astype(BF16)
            forcing = jnp.dot(phys, low, preferred_element_type=F32)
            for i in range(BLOCK_ROWS):
                push = forcing[:, i * LANES : (i + 1) * LANES] + bias
                value = dep[i] + jnp.tanh(push)
                row = band * BLOCK_ROWS + i
                if last:
                    refs[1][pl.ds((row * 5 + tile) * fields, fields), :] = value
                else:
                    put_row(row, rows, (tile,), value.astype(BF16), *refs[:3])
    if last:
        for f in range(fields):
            for t in range(5):
                got = refs[1][pl.ds(t * fields + f, rows, stride=5 * fields), :]
                refs[0][f, :, pl.ds(t * LANES, LANES)] = got.astype(BF16)


def advance(last, params, edges, before, now, after, phys, bias):
    rows, tiles, fields = now.shape[:3]
    smem, vmem = pl.BlockSpec(memory_space=pltpu.SMEM), pl.BlockSpec(memory_space=pltpu.VMEM)
    scratch = [pltpu.VMEM((ABOVE + rows + BELOW, tiles, fields, LANES), BF16)]
    if last:
        shape = jax.ShapeDtypeStruct((fields, rows, 5 * LANES), BF16)
        scratch.insert(0, pltpu.VMEM((rows * 5 * fields, LANES), F32))
    else:
        shape = state_shapes(rows, tiles, fields)
    return pl.pallas_call(
        functools.partial(advance_kernel, last),
        out_shape=shape,
        in_specs=[smem, smem] + [vmem] * 5,
        scratch_shapes=scratch,
        compiler_params=pltpu.CompilerParams(vmem_limit_bytes=16 << 20),
        name="advance_last" if last else "advance_first",
    )(params, edges, before, now, after, phys, bias)


def row_halos(last, first):
    size = lax.axis_size("wave")
    before = lax.ppermute(last, "wave", [(i, i + 1) for i in range(size - 1)])
    after = lax.ppermute(first, "wave", [(i + 1, i) for i in range(size - 1)])
    return before, after


def shards(spectral, wave_ids, lat_rows, shift_rows, shift_cols, frac_rows, frac_cols, phys_weight, phys_bias):
    slots, parts, fields, waves = spectral.shape
    lats = lat_rows.shape[0]
    bands, owners = lax.axis_size("wave"), lax.axis_size("lev")
    nlon = shift_rows.shape[2] * BLOCK_COLS * owners
    scale = 1.0 / math.sqrt(waves)
    band = lax.axis_index("wave").astype(jnp.int32).reshape(1)
    owner = lax.axis_index("lev").astype(jnp.int32).reshape(1)
    outgoing = legendre(
        spectral.reshape(slots * parts * fields, waves), wave_ids, band, lat_rows, 8 * lats, nlon // owners - 1, 2 * nlon, scale
    )
    outgoing = outgoing.reshape(bands, lats // bands, slots * parts * fields)
    arrived = lax.all_to_all(outgoing, "wave", split_axis=0, concat_axis=0, tiled=True)
    table, m, stamp, params = fourier_table(
        wave_ids[None, :], shift_rows, shift_cols, frac_rows, frac_cols, 2 * nlon, 6
    )
    bias = phys_bias[None, :]
    arrived, params, bias = lax.optimization_barrier((arrived, params, bias))
    columns = fourier(arrived, m, stamp, table, scale)
    columns = lax.all_to_all(columns, "lev", split_axis=0, concat_axis=0, tiled=True)
    state, last, first, edges = regroup(columns, owner)
    before, after = row_halos(last, first)
    state, last, first = advance(False, params, edges, before, state, after, phys_weight, bias)
    before, after = row_halos(last, first)
    return advance(True, params, edges, before, state, after, phys_weight, bias)


def solution(mesh):
    blocks = P(None, "wave", "lev")
    return jax.shard_map(
        shards,
        mesh=mesh,
        in_specs=(P("wave", None, "lev", None), P(), P(), blocks, blocks, blocks, blocks, P(), P()),
        out_specs=P(None, "wave", "lev"),
        check_vma=False,
    )
```

```python
import functools
import math

import jax
import jax.numpy as jnp
from jax import lax
from jax.experimental import pallas as pl
from jax.experimental.pallas import tpu as pltpu
from jax.sharding import PartitionSpec as P

BLOCK_ROWS = 4
BLOCK_COLS = 128
LANES = 128
REACH = 6
HALO = 16
STAMP_LANE = 4 * HALO
PER_BLOCK = 10
F32 = jnp.float32
BF16 = jnp.bfloat16
NT = (((1,), (1,)), ((), ()))


def sincos(x, period):
    quarter = period // 4
    turns = jnp.floor(x * (1.0 / quarter) + 0.5)
    t = (x - turns * float(quarter)) * (2.0 * math.pi / period)
    t2 = t * t
    s = t * (1.0 + t2 * (-1.0 / 6.0 + t2 * (1.0 / 120.0 + t2 * (-1.0 / 5040.0))))
    c = 1.0 + t2 * (-0.5 + t2 * (1.0 / 24.0 + t2 * (-1.0 / 720.0 + t2 * (1.0 / 40320.0))))
    k = turns.astype(jnp.int32)
    swap = (k & 1) == 1
    cos, sin = jnp.where(swap, s, c), jnp.where(swap, c, s)
    cos = jnp.where(((k + 1) & 2) != 0, -cos, cos)
    sin = jnp.where((k & 2) != 0, -sin, sin)
    return cos, sin


def rotate(c, s, rc, rs):
    return c * rc - s * rs, s * rc + c * rs


def down(row):
    return jnp.broadcast_to(row, (LANES, LANES)).T


def legendre_kernel(
    period, middle, turn, scale, ids_hbm, lat_hbm, band_ref, x_hbm, out_ref, cos_ref, sin_ref, cw_ref, sw_ref, lat_ref,
    ids_ref, lat_in_ref, x_ref, sems,
):
    loads = [
        pltpu.make_async_copy(src, dst, sems.at[i])
        for i, (src, dst) in enumerate(((ids_hbm, ids_ref), (lat_hbm, lat_in_ref), (x_hbm, x_ref)))
    ]
    for load in loads:
        load.start()
    rows, waves = 4 * x_ref.shape[0], x_ref.shape[3]
    half = waves // 2
    lats = out_ref.shape[0]
    slots = rows // 4
    step = 32
    lane = lax.broadcasted_iota(jnp.int32, (1, LANES), 1)
    first = band_ref[0] * slots
    loads[0].wait()
    m_row = jnp.zeros((1, LANES), jnp.int32)
    for s in range(slots):
        m_row = jnp.where(lane // 4 == s, ids_ref[first + s], m_row)
    m_row = m_row.astype(F32)
    loads[1].wait()
    for i in range(lats // LANES):
        row = lat_in_ref[pl.ds(i * LANES, LANES)].astype(F32).reshape(1, LANES)
        lat_ref[pl.ds(i * LANES, LANES), :] = down(row)
    odd = 2.0 * lax.broadcasted_iota(jnp.int32, (step, LANES), 1).astype(F32) + 1.0
    centre = jnp.broadcast_to(2.0 * m_row + float(waves - 1), (step, LANES))

    def fill(i, carry):
        at = pl.ds(pl.multiple_of(i * step, step), step)
        lat = lat_ref[at, :]
        cw, sw = sincos(lat * centre, 2 * period)
        cw_ref[at, :] = cw
        sw_ref[at, :] = sw
        c, s = sincos(lat * odd, 2 * period)
        rc, rs = sincos(lat * float(LANES), period)
        for a in range(half // LANES):
            cols = pl.ds(a * LANES, LANES)
            cos_ref[at, cols] = c.astype(BF16)
            sin_ref[at, cols] = s.astype(BF16)
            if a + 1 < half // LANES:
                c, s = rotate(c, s, rc, rs)
        return carry

    lax.fori_loop(0, lats // step, fill, 0)
    loads[2].wait()
    m_col = down(m_row)
    k = lax.broadcasted_iota(jnp.int32, (rows, LANES), 1).astype(F32)
    kept = []
    for a in range(waves // LANES):
        part = x_ref[:, :, :, pl.ds(a * LANES, LANES)].astype(F32).reshape(rows, LANES)
        kept.append(jnp.where(k < (waves - a * LANES) - m_col, part, 0.0).astype(BF16))
    src = lax.broadcasted_iota(jnp.int32, (rows, rows), 0)
    dst = lax.broadcasted_iota(jnp.int32, (rows, rows), 1)
    flip = jnp.where(src + dst == LANES - 1, 1.0, 0.0).astype(BF16)
    count = half // LANES
    upper = jnp.concatenate(kept[count:], axis=1)
    lower = jnp.concatenate(
        [jnp.dot(part, flip, preferred_element_type=F32).astype(BF16) for part in kept[count - 1 :: -1]], axis=1
    )
    both = jnp.concatenate([upper, lower], axis=0)
    even = lax.dot_general(cos_ref[...], both, NT, preferred_element_type=F32)
    odds = lax.dot_general(sin_ref[...], both, NT, preferred_element_type=F32)
    even = even[:, :rows] + even[:, rows:]
    odds = odds[:, :rows] - odds[:, rows:]
    leg = (cw_ref[...] * even - sw_ref[...] * odds) * scale
    cos, sin = sincos(m_row * float(middle), turn)
    real = lane % 4 < 2
    other = jnp.where(real, pltpu.roll(leg, LANES - 2, 1), pltpu.roll(leg, 2, 1))
    leg = (leg * cos + other * jnp.where(real, -sin, sin)).astype(BF16)
    order = jnp.where((src % 4) * slots + src // 4 == dst, 1.0, 0.0).astype(BF16)
    out_ref[...] = jnp.dot(leg, order, preferred_element_type=F32).astype(BF16)


def legendre(x, wave_ids, band, lat_rows, period, middle, turn, scale):
    rows, waves = 4 * x.shape[0], x.shape[3]
    lats = lat_rows.shape[0]
    hbm, smem = pl.BlockSpec(memory_space=pltpu.HBM), pl.BlockSpec(memory_space=pltpu.SMEM)
    vmem = pl.BlockSpec(memory_space=pltpu.VMEM)
    return pl.pallas_call(
        functools.partial(legendre_kernel, period, middle, turn, scale),
        out_shape=jax.ShapeDtypeStruct((lats, rows), BF16),
        in_specs=[hbm, hbm, smem, hbm],
        out_specs=vmem,
        scratch_shapes=[
            pltpu.VMEM((lats, waves // 2), BF16),
            pltpu.VMEM((lats, waves // 2), BF16),
            pltpu.VMEM((lats, LANES), F32),
            pltpu.VMEM((lats, LANES), F32),
            pltpu.VMEM((lats, LANES), F32),
            pltpu.SMEM(wave_ids.shape, jnp.int32),
            pltpu.VMEM(lat_rows.shape, jnp.int32),
            pltpu.VMEM(x.shape, BF16),
            pltpu.SemaphoreType.DMA((3,)),
        ],
        compiler_params=pltpu.CompilerParams(vmem_limit_bytes=67043328),
        name="legendre",
    )(wave_ids, lat_rows, band, x)


def times_i(z, power):
    re, im = z
    return ((re, im), (-im, re), (-re, -im), (im, -re))[power % 4]


def add(*terms):
    re, im = terms[0]
    for r, i in terms[1:]:
        re, im = re + r, im + i
    return re, im


def four(z):
    a, b = add(z[0], z[2]), add(z[0], times_i(z[2], 2))
    c, d = add(z[1], z[3]), add(z[1], times_i(z[3], 2))
    return add(a, c), add(b, times_i(d, 1)), add(a, times_i(c, 2)), add(b, times_i(d, 3))


def sixteen_real(y):
    inner = [four([y[4 * q1 + q0] for q1 in range(4)]) for q0 in range(4)]
    out = [None] * 16
    for a0 in range(4):
        v = []
        for q0 in range(4):
            re, im = inner[q0][a0]
            if q0 * a0:
                angle = 2.0 * math.pi * q0 * a0 / 16.0
                cos, sin = math.cos(angle), math.sin(angle)
                re, im = re * cos - im * sin, re * sin + im * cos
            v.append((re, im))
        even, odd = v[0][0] + v[2][0], v[0][0] - v[2][0]
        plus, minus = v[1][0] + v[3][0], v[3][1] - v[1][1]
        out[a0], out[a0 + 8] = even + plus, even - plus
        out[a0 + 4], out[a0 + 12] = odd + minus, odd - minus
    return out


def cubic_weights(fraction):
    coord = 1.0 - fraction
    return (
        -coord * (coord - 1.0) * (coord - 2.0) * (1.0 / 6.0),
        (coord + 1.0) * (coord - 1.0) * (coord - 2.0) * 0.5,
        -(coord + 1.0) * coord * (coord - 2.0) * 0.5,
        (coord + 1.0) * coord * (coord - 1.0) * (1.0 / 6.0),
    )


def table_kernel(period, ids_ref, sr_ref, sc_ref, fr_ref, fc_ref, e_ref, m_ref, stamp_ref, param_ref):
    waves = ids_ref.shape[1]
    spans = e_ref.shape[0] // LANES
    odd = 2.0 * lax.broadcasted_iota(jnp.int32, (8, LANES), 0).astype(F32) + 1.0
    m_ref[...] = ids_ref[...].astype(F32)

    def fill(i, carry):
        at = pl.ds(pl.multiple_of(i * LANES, LANES), LANES)
        m = jnp.broadcast_to(ids_ref[:, at].astype(F32), (8, LANES))
        c8, s8 = sincos(m * 16.0, period)
        c64, s64 = sincos(m * 128.0, period)
        z = [sincos(m * odd, period)]
        for _ in range(7):
            z.append(rotate(*z[-1], c8, s8))
        for t in range(spans):
            base = 256 * (t // 2) + 64 * (t % 2)
            for h in range(4):
                (c0, s0), (c1, s1) = z[2 * h], z[2 * h + 1]
                e_ref[pl.ds(base + h * 16, 16), at] = jnp.concatenate([c0, c1], axis=0).astype(BF16)
                e_ref[pl.ds(base + 128 + h * 16, 16), at] = jnp.concatenate([s0, s1], axis=0).astype(BF16)
            if t + 1 < spans:
                z = [rotate(a, b, c64, s64) for a, b in z]
        return carry

    lax.fori_loop(0, waves // LANES, fill, 0)
    steps, bands, blocks = sr_ref.shape
    lane = lax.broadcasted_iota(jnp.int32, (8, LANES), 1)
    row = lax.broadcasted_iota(jnp.int32, (8, LANES), 0)
    stamp = jnp.zeros((8, LANES), F32)
    for step in range(steps):
        for band in range(bands):
            for block in range(blocks):
                moves = (sr_ref[step, band, block].astype(F32), sc_ref[step, band, block].astype(F32))
                values = moves + cubic_weights(fr_ref[step, band, block]) + cubic_weights(fc_ref[step, band, block])
                for k, value in enumerate(values):
                    param_ref[((step * bands + band) * blocks + block) * PER_BLOCK + k] = value
                    side = {0: 0, blocks - 1: 1}.get(block)
                    if step == 0 and side is not None:
                        at = STAMP_LANE + (side * bands + band) * PER_BLOCK + k
                        stamp = jnp.where(lane == at, value, stamp)
    high = stamp.astype(BF16).astype(F32)
    mid = (stamp - high).astype(BF16).astype(F32)
    stamp_ref[...] = jnp.where(row == 0, high, jnp.where(row == 1, mid, jnp.where(row == 2, stamp - high - mid, 0.0)))


def fourier_table(ids, shift_rows, shift_cols, frac_rows, frac_cols, period, tiles):
    waves = ids.shape[1]
    smem, vmem = pl.BlockSpec(memory_space=pltpu.SMEM), pl.BlockSpec(memory_space=pltpu.VMEM)
    return pl.pallas_call(
        functools.partial(table_kernel, period),
        out_shape=[
            jax.ShapeDtypeStruct((tiles * LANES, waves), BF16),
            jax.ShapeDtypeStruct((1, waves), F32),
            jax.ShapeDtypeStruct((8, LANES), F32),
            jax.ShapeDtypeStruct((shift_rows.size * PER_BLOCK,), F32),
        ],
        in_specs=[vmem] + [smem] * 4,
        out_specs=[vmem, vmem, vmem, smem],
        compiler_params=pltpu.CompilerParams(vmem_limit_bytes=8 << 20),
        cost_estimate=pl.CostEstimate(flops=20000000, bytes_accessed=2500000, transcendentals=0),
        name="fourier_table",
    )(ids, shift_rows, shift_cols, frac_rows, frac_cols)


def fourier_kernel(scale, z_ref, m_ref, stamp_ref, e_ref, out_ref, l_ref, d_ref, g_ref):
    waves = m_ref.shape[1]
    group = lax.broadcasted_iota(jnp.int32, (8, LANES), 1) // 32

    def spread(i, carry):
        at = pl.ds(pl.multiple_of(i * LANES, LANES), LANES)
        block = [z_ref[4 * i + u].astype(F32) for u in range(4)]
        parts = []
        for cf in range(4):
            whole = None
            for u in range(4):
                turn = (32 * (u - cf)) % LANES
                moved = pltpu.roll(block[u], turn, 1) if turn else block[u]
                whole = moved if whole is None else jnp.where(group == u, moved, whole)
            parts.append(whole)
        both = jnp.concatenate(parts, axis=0)
        m = jnp.broadcast_to(m_ref[:, at], both.shape)
        residue = m - 16.0 * jnp.floor(m * 0.0625)
        for q in range(16):
            l_ref[pl.ds(q * 32, 32), at] = jnp.where(residue == float(q), both, 0.0).astype(BF16)
        return carry

    lax.fori_loop(0, waves // LANES, spread, 0)
    halves = e_ref.shape[0] // 256
    low, high = pl.ds(0, LANES), pl.ds(LANES, LANES)
    for p in range(halves):
        d_ref[...] = lax.dot_general(l_ref[...], e_ref[pl.ds(p * 256, 256), :], NT, preferred_element_type=F32)
        right, left = [], []
        for q in range(16):
            re, im = pl.ds(q * 32, 16), pl.ds(q * 32 + 16, 16)
            c0, c1, s0, s1 = d_ref[re, low], d_ref[im, low], d_ref[re, high], d_ref[im, high]
            right.append((c0 - s1, c1 + s0))
            left.append((c0 + s1, c1 - s0))
        for side, y in ((halves + p, right), (halves - 1 - p, left)):
            for a, value in enumerate(sixteen_real(y)):
                g_ref[side, pl.ds(a * 16, 16), :] = (value * scale).astype(BF16)

    src = lax.broadcasted_iota(jnp.int32, (LANES, LANES), 0)
    dst = lax.broadcasted_iota(jnp.int32, (LANES, LANES), 1)
    half = LANES // 2

    def pick(mirrored, upper):
        want = (half - 1 + LANES * upper - dst) if mirrored else (dst + half - LANES * upper)
        inside = (dst >= half) if upper else (dst < half)
        return jnp.where(inside & (src == want), 1.0, 0.0).astype(BF16)

    lane = lax.broadcasted_iota(jnp.int32, (8, LANES), 1)
    stamp = stamp_ref[...]
    tiles = 2 * halves
    for t in range(tiles):
        first, second = t, (t + 1) % tiles
        value = jnp.dot(g_ref[first], pick(first < halves, 0), preferred_element_type=F32) + jnp.dot(
            g_ref[second], pick(second < halves, 1), preferred_element_type=F32
        )
        for a in range(16):
            one, two = value[a * 16 : a * 16 + 8], value[a * 16 + 8 : a * 16 + 16]
            if t < tiles - 1:
                out_ref[a, pl.ds(t * 8, 8), :] = one.astype(BF16)
                out_ref[a, pl.ds((tiles - 1 + t) * 8, 8), :] = two.astype(BF16)
            else:
                one, two = pltpu.roll(one, HALO, 1), pltpu.roll(two, 3 * HALO, 1)
                halo = jnp.where(lane < 2 * HALO, one, jnp.where(lane < STAMP_LANE, two, stamp))
                out_ref[a, pl.ds((tiles - 1) * 16, 8), :] = halo.astype(BF16)


def fourier(z, m, stamp, table, scale):
    tiles = table.shape[0] // LANES
    vmem = pl.BlockSpec(memory_space=pltpu.VMEM)
    return pl.pallas_call(
        functools.partial(fourier_kernel, scale),
        out_shape=jax.ShapeDtypeStruct((16, tiles * 16 - 8, LANES), BF16),
        in_specs=[vmem] * 4,
        out_specs=vmem,
        scratch_shapes=[
            pltpu.VMEM((512, table.shape[1]), BF16),
            pltpu.VMEM((512, 256), F32),
            pltpu.VMEM((tiles, 256, LANES), BF16),
        ],
        compiler_params=pltpu.CompilerParams(vmem_limit_bytes=24 << 20),
        name="fourier",
    )(z, m, stamp, table)


def sent_start(rows, odd, side):
    return odd * (rows - REACH) if side else (1 - odd) * (rows - REACH)


def got_start(rows, odd, side):
    return odd * (rows + REACH) if side else (1 - odd) * (rows + REACH)


def state_shapes(rows, tiles, fields):
    return [jax.ShapeDtypeStruct((n, tiles, fields, LANES), BF16) for n in (rows, REACH, REACH)]


def regroup_kernel(owner_ref, odd_ref, x_ref, out_ref, near_ref, far_ref, edge_ref, wide_ref):
    rows, tiles, fields = out_ref.shape[:3]
    sources = x_ref.shape[0]
    main, span = (tiles - 1) * rows, tiles * rows
    for v in range(sources):
        halo = x_ref[v, pl.ds(2 * main, rows), :].astype(F32)
        for f in range(2):
            at = (2 * v + f) * span
            wide_ref[pl.ds(at, main), :] = x_ref[v, pl.ds(f * main, main), :].astype(F32)
            wide_ref[pl.ds(at + main, rows), :] = pltpu.roll(halo, LANES - HALO - 2 * HALO * f, 1)
    for j in range(rows):
        for t in range(tiles):
            got = wide_ref[pl.ds(t * rows + j, fields, stride=span), :]
            out_ref[j, t] = got.astype(BF16)
    for side, ref in enumerate((near_ref, far_ref)):
        ref[...] = out_ref[pl.ds(sent_start(rows, odd_ref[0], side), REACH)]
    owner = owner_ref[0]
    edges = []
    for source in ((owner + sources - 1) % sources, (owner + 1) % sources):
        parts = x_ref[source, pl.ds(2 * main, rows), :].astype(F32)
        edges.append(parts[0:1] + parts[1:2] + parts[2:3])
    edge_ref[...] = jnp.concatenate(edges, axis=0)


def regroup(x, owner, odd):
    smem, vmem = pl.BlockSpec(memory_space=pltpu.SMEM), pl.BlockSpec(memory_space=pltpu.VMEM)
    tiles = (x.shape[1] + 8) // 16
    return pl.pallas_call(
        regroup_kernel,
        out_shape=state_shapes(8, tiles, 32) + [jax.ShapeDtypeStruct((2, LANES), F32)],
        in_specs=[smem, smem, vmem],
        out_specs=[vmem] * 4,
        scratch_shapes=[pltpu.VMEM((32 * tiles * 8, LANES), F32)],
        compiler_params=pltpu.CompilerParams(vmem_limit_bytes=8 << 20),
        name="regroup",
    )(owner, odd, x)


def advance_kernel(last, param_ref, edge_ref, odd_ref, near_ref, now_ref, far_ref, phys_ref, bias_ref, *refs):
    rows, tiles, fields = now_ref.shape[:3]
    s_ref = refs[-1]
    odd = odd_ref[0]
    s_ref[pl.ds(REACH, rows)] = now_ref[...]
    for side, ref in enumerate((near_ref, far_ref)):
        s_ref[pl.ds(got_start(rows, odd, side), REACH)] = ref[...]
    bands = rows // BLOCK_ROWS
    lane = lax.broadcasted_iota(jnp.int32, (fields, LANES), 1)
    left_half = lane < LANES // 2
    phys = phys_ref[...]
    bias = jnp.broadcast_to(bias_ref[...], (LANES, fields)).T

    def departed(band, block, tile):
        if 0 <= block < 5:
            start = ((last * bands + band) * 5 + block) * PER_BLOCK
            value = [param_ref[start + k] for k in range(PER_BLOCK)]
        else:
            west = block < 0
            start = STAMP_LANE + (west * bands + band) * PER_BLOCK
            value = [edge_ref[0 if west else 1, start + k] for k in range(PER_BLOCK)]
        base = REACH - 2 + band * BLOCK_ROWS - value[0].astype(jnp.int32)
        first = -value[1].astype(jnp.int32) - 2
        wr, wc = value[2:6], value[6:10]
        centre, edge = [], []
        for k in range(BLOCK_ROWS + 3):
            before = s_ref[base + k, (tile + tiles - 1) % tiles].astype(F32)
            after = s_ref[base + k, (tile + 1) % tiles].astype(F32)
            centre.append(s_ref[base + k, tile].astype(F32))
            edge.append(jnp.where(left_half, after, before))
        taps = []
        for b in range(4):
            shift = first + b
            outside = (lane < shift) | (lane >= LANES + shift)
            taps.append((outside, (LANES - shift) & (LANES - 1)))
        result = []
        for i in range(BLOCK_ROWS):
            c = sum(wr[a] * centre[i + a] for a in range(4))
            e = sum(wr[a] * edge[i + a] for a in range(4))
            total = None
            for b in range(4):
                outside, turn = taps[b]
                term = wc[b] * pltpu.roll(jnp.where(outside, e, c), turn, 1)
                total = term if total is None else total + term
            result.append(total)
        return result

    for band in range(bands):
        for tile in range(5 if last else 6):
            if tile < 5:
                dep = departed(band, tile, tile)
            else:
                right = departed(band, 5, tile)
                left = departed(band, -1, tile)
                dep = [jnp.where(left_half, r, l) for r, l in zip(right, left)]
            low = jnp.concatenate(dep, axis=1).astype(BF16)
            forcing = jnp.dot(phys, low, preferred_element_type=F32)
            for i in range(BLOCK_ROWS):
                push = forcing[:, i * LANES : (i + 1) * LANES] + bias
                value = dep[i] + jnp.tanh(push)
                row = band * BLOCK_ROWS + i
                if last:
                    refs[1][pl.ds((row * 5 + tile) * fields, fields), :] = value
                else:
                    refs[0][row, tile] = value.astype(BF16)
    if not last:
        for side in range(2):
            refs[1 + side][...] = refs[0][pl.ds(sent_start(rows, odd, side), REACH)]
    if last:
        for f in range(fields):
            for t in range(5):
                got = refs[1][pl.ds(t * fields + f, rows, stride=5 * fields), :]
                refs[0][f, :, pl.ds(t * LANES, LANES)] = got.astype(BF16)


def advance(last, params, edges, odd, near, now, far, phys, bias):
    rows, tiles, fields = now.shape[:3]
    smem, vmem = pl.BlockSpec(memory_space=pltpu.SMEM), pl.BlockSpec(memory_space=pltpu.VMEM)
    scratch = [pltpu.VMEM((rows + 2 * REACH, tiles, fields, LANES), BF16)]
    if last:
        shape = jax.ShapeDtypeStruct((fields, rows, 5 * LANES), BF16)
        scratch.insert(0, pltpu.VMEM((rows * 5 * fields, LANES), F32))
    else:
        shape = state_shapes(rows, tiles, fields)
    return pl.pallas_call(
        functools.partial(advance_kernel, last),
        out_shape=shape,
        in_specs=[smem] * 3 + [vmem] * 5,
        scratch_shapes=scratch,
        compiler_params=pltpu.CompilerParams(vmem_limit_bytes=16 << 20),
        name="advance_last" if last else "advance_first",
    )(params, edges, odd, near, now, far, phys, bias)


def row_halos(near, far):
    size = lax.axis_size("wave")
    pairs = [(i + d, i + 1 - d) for i in range(size - 1) for d in (0, 1)]
    far = lax.ppermute(far, "wave", [p for p in pairs if min(p) % 2])
    near = lax.ppermute(near, "wave", [p for p in pairs if not min(p) % 2])
    return near, far


def shards(spectral, wave_ids, lat_rows, shift_rows, shift_cols, frac_rows, frac_cols, phys_weight, phys_bias):
    slots, parts, fields, waves = spectral.shape
    lats = lat_rows.shape[0]
    bands, owners = lax.axis_size("wave"), lax.axis_size("lev")
    nlon = shift_rows.shape[2] * BLOCK_COLS * owners
    scale = 1.0 / math.sqrt(waves)
    band = lax.axis_index("wave").astype(jnp.int32).reshape(1)
    owner = lax.axis_index("lev").astype(jnp.int32).reshape(1)
    outgoing = legendre(
        spectral, wave_ids, band, lat_rows, 8 * lats, nlon // owners - 1, 2 * nlon, scale
    )
    outgoing = outgoing.reshape(bands, lats // bands, slots * parts * fields)
    arrived = lax.all_to_all(outgoing, "wave", split_axis=0, concat_axis=0, tiled=True)
    table, m, stamp, params = fourier_table(
        wave_ids[None, :], shift_rows, shift_cols, frac_rows, frac_cols, 2 * nlon, 6
    )
    bias = phys_bias[None, :]
    arrived, params, bias = lax.optimization_barrier((arrived, params, bias))
    columns = fourier(arrived, m, stamp, table, scale)
    columns = lax.all_to_all(columns, "lev", split_axis=0, concat_axis=0, tiled=True)
    odd = band % 2
    state, near, far, edges = regroup(columns, owner, odd)
    near, far = row_halos(near, far)
    state, near, far = advance(False, params, edges, odd, near, state, far, phys_weight, bias)
    near, far = row_halos(near, far)
    return advance(True, params, edges, odd, near, state, far, phys_weight, bias)


def solution(mesh):
    blocks = P(None, "wave", "lev")
    return jax.shard_map(
        shards,
        mesh=mesh,
        in_specs=(P("wave", None, "lev", None), P(), P(), blocks, blocks, blocks, blocks, P(), P()),
        out_specs=P(None, "wave", "lev"),
        check_vma=False,
    )
```

```python
import functools
import math

import jax
import jax.numpy as jnp
from jax import lax
from jax.experimental import pallas as pl
from jax.experimental.pallas import tpu as pltpu
from jax.sharding import PartitionSpec as P

BLOCK_ROWS = 4
BLOCK_COLS = 128
LANES = 128
ABOVE = 6
BELOW = 5
HALO = 16
STAMP_LANE = 4 * HALO
PER_BLOCK = 10
F32 = jnp.float32
BF16 = jnp.bfloat16
NT = (((1,), (1,)), ((), ()))


def sincos(x, period):
    quarter = period // 4
    turns = jnp.floor(x * (1.0 / quarter) + 0.5)
    t = (x - turns * float(quarter)) * (2.0 * math.pi / period)
    t2 = t * t
    s = t * (1.0 + t2 * (-1.0 / 6.0 + t2 * (1.0 / 120.0 + t2 * (-1.0 / 5040.0))))
    c = 1.0 + t2 * (-0.5 + t2 * (1.0 / 24.0 + t2 * (-1.0 / 720.0 + t2 * (1.0 / 40320.0))))
    k = turns.astype(jnp.int32)
    swap = (k & 1) == 1
    cos, sin = jnp.where(swap, s, c), jnp.where(swap, c, s)
    cos = jnp.where(((k + 1) & 2) != 0, -cos, cos)
    sin = jnp.where((k & 2) != 0, -sin, sin)
    return cos, sin


def rotate(c, s, rc, rs):
    return c * rc - s * rs, s * rc + c * rs


def down(row):
    return jnp.broadcast_to(row, (LANES, LANES)).T


def legendre_kernel(
    period, middle, turn, scale, ids_hbm, lat_hbm, band_ref, x_hbm, out_ref, cos_ref, sin_ref, cw_ref, sw_ref, lat_ref,
    ids_ref, lat_in_ref, x_ref, sems,
):
    loads = [
        pltpu.make_async_copy(src, dst, sems.at[i])
        for i, (src, dst) in enumerate(((ids_hbm, ids_ref), (lat_hbm, lat_in_ref), (x_hbm, x_ref)))
    ]
    for load in loads:
        load.start()
    rows, waves = 4 * x_ref.shape[0], x_ref.shape[3]
    half = waves // 2
    lats = out_ref.shape[0]
    slots = rows // 4
    step = 32
    lane = lax.broadcasted_iota(jnp.int32, (1, LANES), 1)
    first = band_ref[0] * slots
    loads[0].wait()
    m_row = jnp.zeros((1, LANES), jnp.int32)
    for s in range(slots):
        m_row = jnp.where(lane // 4 == s, ids_ref[first + s], m_row)
    m_row = m_row.astype(F32)
    loads[1].wait()
    for i in range(lats // LANES):
        row = lat_in_ref[pl.ds(i * LANES, LANES)].astype(F32).reshape(1, LANES)
        lat_ref[pl.ds(i * LANES, LANES), :] = down(row)
    odd = 2.0 * lax.broadcasted_iota(jnp.int32, (step, LANES), 1).astype(F32) + 1.0
    centre = jnp.broadcast_to(2.0 * m_row + float(waves - 1), (step, LANES))

    def fill(i, carry):
        at = pl.ds(pl.multiple_of(i * step, step), step)
        lat = lat_ref[at, :]
        cw, sw = sincos(lat * centre, 2 * period)
        cw_ref[at, :] = cw
        sw_ref[at, :] = sw
        c, s = sincos(lat * odd, 2 * period)
        rc, rs = sincos(lat * float(LANES), period)
        for a in range(half // LANES):
            cols = pl.ds(a * LANES, LANES)
            cos_ref[at, cols] = c.astype(BF16)
            sin_ref[at, cols] = s.astype(BF16)
            if a + 1 < half // LANES:
                c, s = rotate(c, s, rc, rs)
        return carry

    lax.fori_loop(0, lats // step, fill, 0)
    loads[2].wait()
    m_col = down(m_row)
    k = lax.broadcasted_iota(jnp.int32, (rows, LANES), 1).astype(F32)
    kept = []
    for a in range(waves // LANES):
        part = x_ref[:, :, :, pl.ds(a * LANES, LANES)].astype(F32).reshape(rows, LANES)
        kept.append(jnp.where(k < (waves - a * LANES) - m_col, part, 0.0).astype(BF16))
    src = lax.broadcasted_iota(jnp.int32, (rows, rows), 0)
    dst = lax.broadcasted_iota(jnp.int32, (rows, rows), 1)
    flip = jnp.where(src + dst == LANES - 1, 1.0, 0.0).astype(BF16)
    count = half // LANES
    upper = jnp.concatenate(kept[count:], axis=1)
    lower = jnp.concatenate(
        [jnp.dot(part, flip, preferred_element_type=F32).astype(BF16) for part in kept[count - 1 :: -1]], axis=1
    )
    both = jnp.concatenate([upper, lower], axis=0)
    even = lax.dot_general(cos_ref[...], both, NT, preferred_element_type=F32)
    odds = lax.dot_general(sin_ref[...], both, NT, preferred_element_type=F32)
    even = even[:, :rows] + even[:, rows:]
    odds = odds[:, :rows] - odds[:, rows:]
    leg = (cw_ref[...] * even - sw_ref[...] * odds) * scale
    cos, sin = sincos(m_row * float(middle), turn)
    real = lane % 4 < 2
    other = jnp.where(real, pltpu.roll(leg, LANES - 2, 1), pltpu.roll(leg, 2, 1))
    leg = (leg * cos + other * jnp.where(real, -sin, sin)).astype(BF16)
    order = jnp.where((src % 4) * slots + src // 4 == dst, 1.0, 0.0).astype(BF16)
    out_ref[...] = jnp.dot(leg, order, preferred_element_type=F32).astype(BF16)


def legendre(x, wave_ids, band, lat_rows, period, middle, turn, scale):
    rows, waves = 4 * x.shape[0], x.shape[3]
    lats = lat_rows.shape[0]
    hbm, smem = pl.BlockSpec(memory_space=pltpu.HBM), pl.BlockSpec(memory_space=pltpu.SMEM)
    vmem = pl.BlockSpec(memory_space=pltpu.VMEM)
    return pl.pallas_call(
        functools.partial(legendre_kernel, period, middle, turn, scale),
        out_shape=jax.ShapeDtypeStruct((lats, rows), BF16),
        in_specs=[hbm, hbm, smem, hbm],
        out_specs=vmem,
        scratch_shapes=[
            pltpu.VMEM((lats, waves // 2), BF16),
            pltpu.VMEM((lats, waves // 2), BF16),
            pltpu.VMEM((lats, LANES), F32),
            pltpu.VMEM((lats, LANES), F32),
            pltpu.VMEM((lats, LANES), F32),
            pltpu.SMEM(wave_ids.shape, jnp.int32),
            pltpu.VMEM(lat_rows.shape, jnp.int32),
            pltpu.VMEM(x.shape, BF16),
            pltpu.SemaphoreType.DMA((3,)),
        ],
        compiler_params=pltpu.CompilerParams(vmem_limit_bytes=67043328),
        name="legendre",
    )(wave_ids, lat_rows, band, x)


def times_i(z, power):
    re, im = z
    return ((re, im), (-im, re), (-re, -im), (im, -re))[power % 4]


def add(*terms):
    re, im = terms[0]
    for r, i in terms[1:]:
        re, im = re + r, im + i
    return re, im


def four(z):
    a, b = add(z[0], z[2]), add(z[0], times_i(z[2], 2))
    c, d = add(z[1], z[3]), add(z[1], times_i(z[3], 2))
    return add(a, c), add(b, times_i(d, 1)), add(a, times_i(c, 2)), add(b, times_i(d, 3))


def sixteen_real(y):
    inner = [four([y[4 * q1 + q0] for q1 in range(4)]) for q0 in range(4)]
    out = [None] * 16
    for a0 in range(4):
        v = []
        for q0 in range(4):
            re, im = inner[q0][a0]
            if q0 * a0:
                angle = 2.0 * math.pi * q0 * a0 / 16.0
                cos, sin = math.cos(angle), math.sin(angle)
                re, im = re * cos - im * sin, re * sin + im * cos
            v.append((re, im))
        even, odd = v[0][0] + v[2][0], v[0][0] - v[2][0]
        plus, minus = v[1][0] + v[3][0], v[3][1] - v[1][1]
        out[a0], out[a0 + 8] = even + plus, even - plus
        out[a0 + 4], out[a0 + 12] = odd + minus, odd - minus
    return out


def cubic_weights(fraction):
    coord = 1.0 - fraction
    return (
        -coord * (coord - 1.0) * (coord - 2.0) * (1.0 / 6.0),
        (coord + 1.0) * (coord - 1.0) * (coord - 2.0) * 0.5,
        -(coord + 1.0) * coord * (coord - 2.0) * 0.5,
        (coord + 1.0) * coord * (coord - 1.0) * (1.0 / 6.0),
    )


def table_kernel(period, ids_ref, sr_ref, sc_ref, fr_ref, fc_ref, e_ref, m_ref, stamp_ref, param_ref):
    waves = ids_ref.shape[1]
    spans = e_ref.shape[0] // LANES
    odd = 2.0 * lax.broadcasted_iota(jnp.int32, (8, LANES), 0).astype(F32) + 1.0
    m_ref[...] = ids_ref[...].astype(F32)

    def fill(i, carry):
        at = pl.ds(pl.multiple_of(i * LANES, LANES), LANES)
        m = jnp.broadcast_to(ids_ref[:, at].astype(F32), (8, LANES))
        c8, s8 = sincos(m * 16.0, period)
        c64, s64 = sincos(m * 128.0, period)
        z = [sincos(m * odd, period)]
        for _ in range(7):
            z.append(rotate(*z[-1], c8, s8))
        for t in range(spans):
            base = 256 * (t // 2) + 64 * (t % 2)
            for h in range(4):
                (c0, s0), (c1, s1) = z[2 * h], z[2 * h + 1]
                e_ref[pl.ds(base + h * 16, 16), at] = jnp.concatenate([c0, c1], axis=0).astype(BF16)
                e_ref[pl.ds(base + 128 + h * 16, 16), at] = jnp.concatenate([s0, s1], axis=0).astype(BF16)
            if t + 1 < spans:
                z = [rotate(a, b, c64, s64) for a, b in z]
        return carry

    lax.fori_loop(0, waves // LANES, fill, 0)
    steps, bands, blocks = sr_ref.shape
    lane = lax.broadcasted_iota(jnp.int32, (8, LANES), 1)
    row = lax.broadcasted_iota(jnp.int32, (8, LANES), 0)
    stamp = jnp.zeros((8, LANES), F32)
    for step in range(steps):
        for band in range(bands):
            for block in range(blocks):
                moves = (sr_ref[step, band, block].astype(F32), sc_ref[step, band, block].astype(F32))
                values = moves + cubic_weights(fr_ref[step, band, block]) + cubic_weights(fc_ref[step, band, block])
                for k, value in enumerate(values):
                    param_ref[((step * bands + band) * blocks + block) * PER_BLOCK + k] = value
                    side = {0: 0, blocks - 1: 1}.get(block)
                    if step == 0 and side is not None:
                        at = STAMP_LANE + (side * bands + band) * PER_BLOCK + k
                        stamp = jnp.where(lane == at, value, stamp)
    high = stamp.astype(BF16).astype(F32)
    mid = (stamp - high).astype(BF16).astype(F32)
    stamp_ref[...] = jnp.where(row == 0, high, jnp.where(row == 1, mid, jnp.where(row == 2, stamp - high - mid, 0.0)))


def fourier_table(ids, shift_rows, shift_cols, frac_rows, frac_cols, period, tiles):
    waves = ids.shape[1]
    smem, vmem = pl.BlockSpec(memory_space=pltpu.SMEM), pl.BlockSpec(memory_space=pltpu.VMEM)
    return pl.pallas_call(
        functools.partial(table_kernel, period),
        out_shape=[
            jax.ShapeDtypeStruct((tiles * LANES, waves), BF16),
            jax.ShapeDtypeStruct((1, waves), F32),
            jax.ShapeDtypeStruct((8, LANES), F32),
            jax.ShapeDtypeStruct((shift_rows.size * PER_BLOCK,), F32),
        ],
        in_specs=[vmem] + [smem] * 4,
        out_specs=[vmem, vmem, vmem, smem],
        compiler_params=pltpu.CompilerParams(vmem_limit_bytes=8 << 20),
        cost_estimate=pl.CostEstimate(flops=20000000, bytes_accessed=2500000, transcendentals=0),
        name="fourier_table",
    )(ids, shift_rows, shift_cols, frac_rows, frac_cols)


def fourier_kernel(scale, z_ref, m_ref, stamp_ref, e_ref, out_ref, l_ref, d_ref, g_ref):
    waves = m_ref.shape[1]
    group = lax.broadcasted_iota(jnp.int32, (8, LANES), 1) // 32

    def spread(i, carry):
        at = pl.ds(pl.multiple_of(i * LANES, LANES), LANES)
        block = [z_ref[4 * i + u].astype(F32) for u in range(4)]
        parts = []
        for cf in range(4):
            whole = None
            for u in range(4):
                turn = (32 * (u - cf)) % LANES
                moved = pltpu.roll(block[u], turn, 1) if turn else block[u]
                whole = moved if whole is None else jnp.where(group == u, moved, whole)
            parts.append(whole)
        both = jnp.concatenate(parts, axis=0)
        m = jnp.broadcast_to(m_ref[:, at], both.shape)
        residue = m - 16.0 * jnp.floor(m * 0.0625)
        for q in range(16):
            l_ref[pl.ds(q * 32, 32), at] = jnp.where(residue == float(q), both, 0.0).astype(BF16)
        return carry

    lax.fori_loop(0, waves // LANES, spread, 0)
    halves = e_ref.shape[0] // 256
    low, high = pl.ds(0, LANES), pl.ds(LANES, LANES)
    for p in range(halves):
        d_ref[...] = lax.dot_general(l_ref[...], e_ref[pl.ds(p * 256, 256), :], NT, preferred_element_type=F32)
        right, left = [], []
        for q in range(16):
            re, im = pl.ds(q * 32, 16), pl.ds(q * 32 + 16, 16)
            c0, c1, s0, s1 = d_ref[re, low], d_ref[im, low], d_ref[re, high], d_ref[im, high]
            right.append((c0 - s1, c1 + s0))
            left.append((c0 + s1, c1 - s0))
        for side, y in ((halves + p, right), (halves - 1 - p, left)):
            for a, value in enumerate(sixteen_real(y)):
                g_ref[side, pl.ds(a * 16, 16), :] = (value * scale).astype(BF16)

    src = lax.broadcasted_iota(jnp.int32, (LANES, LANES), 0)
    dst = lax.broadcasted_iota(jnp.int32, (LANES, LANES), 1)
    half = LANES // 2

    def pick(mirrored, upper):
        want = (half - 1 + LANES * upper - dst) if mirrored else (dst + half - LANES * upper)
        inside = (dst >= half) if upper else (dst < half)
        return jnp.where(inside & (src == want), 1.0, 0.0).astype(BF16)

    lane = lax.broadcasted_iota(jnp.int32, (8, LANES), 1)
    stamp = stamp_ref[...]
    tiles = 2 * halves
    for t in range(tiles):
        first, second = t, (t + 1) % tiles
        value = jnp.dot(g_ref[first], pick(first < halves, 0), preferred_element_type=F32) + jnp.dot(
            g_ref[second], pick(second < halves, 1), preferred_element_type=F32
        )
        for a in range(16):
            one, two = value[a * 16 : a * 16 + 8], value[a * 16 + 8 : a * 16 + 16]
            if t < tiles - 1:
                out_ref[a, pl.ds(t * 8, 8), :] = one.astype(BF16)
                out_ref[a, pl.ds((tiles - 1 + t) * 8, 8), :] = two.astype(BF16)
            else:
                one, two = pltpu.roll(one, HALO, 1), pltpu.roll(two, 3 * HALO, 1)
                halo = jnp.where(lane < 2 * HALO, one, jnp.where(lane < STAMP_LANE, two, stamp))
                out_ref[a, pl.ds((tiles - 1) * 16, 8), :] = halo.astype(BF16)


def fourier(z, m, stamp, table, scale):
    tiles = table.shape[0] // LANES
    vmem = pl.BlockSpec(memory_space=pltpu.VMEM)
    return pl.pallas_call(
        functools.partial(fourier_kernel, scale),
        out_shape=jax.ShapeDtypeStruct((16, tiles * 16 - 8, LANES), BF16),
        in_specs=[vmem] * 4,
        out_specs=vmem,
        scratch_shapes=[
            pltpu.VMEM((512, table.shape[1]), BF16),
            pltpu.VMEM((512, 256), F32),
            pltpu.VMEM((tiles, 256, LANES), BF16),
        ],
        compiler_params=pltpu.CompilerParams(vmem_limit_bytes=24 << 20),
        name="fourier",
    )(z, m, stamp, table)


def send_rows(state_ref, first, sent_ref):
    fields = state_ref.shape[2]
    lane = lax.broadcasted_iota(jnp.int32, (8, LANES), 1)
    for r in range(sent_ref.shape[0]):
        for t in range(5):
            sent_ref[r, pl.ds(t * fields, fields)] = state_ref[first + r, t]
        halo = state_ref[first + r, 5].astype(F32)
        packed = pltpu.roll(halo[0:8], HALO, 1)
        for g in range(1, fields // 8):
            packed = jnp.where(lane < 2 * HALO * g, packed, pltpu.roll(halo[8 * g : 8 * g + 8], HALO * (2 * g + 1), 1))
        sent_ref[r, pl.ds(5 * fields, 8)] = packed.astype(BF16)


def take_rows(got_ref, first, state_ref):
    fields = state_ref.shape[2]
    for r in range(got_ref.shape[0]):
        for t in range(5):
            state_ref[first + r, t] = got_ref[r, pl.ds(t * fields, fields)]
        packed = got_ref[r, pl.ds(5 * fields, 8)].astype(F32)
        halo = [pltpu.roll(packed, (LANES - HALO * (2 * g + 1)) % LANES, 1) for g in range(fields // 8)]
        state_ref[first + r, 5] = jnp.concatenate(halo, axis=0).astype(BF16)


def state_shapes(rows, tiles, fields):
    shapes = [(rows, tiles, fields, LANES)] + [(n, 5 * fields + 8, LANES) for n in (ABOVE, BELOW)]
    return [jax.ShapeDtypeStruct(shape, BF16) for shape in shapes]


def regroup_kernel(owner_ref, x_ref, out_ref, last_ref, first_ref, edge_ref, wide_ref):
    rows, tiles, fields = out_ref.shape[:3]
    sources = x_ref.shape[0]
    main, span = (tiles - 1) * rows, tiles * rows
    for v in range(sources):
        halo = x_ref[v, pl.ds(2 * main, rows), :].astype(F32)
        for f in range(2):
            at = (2 * v + f) * span
            wide_ref[pl.ds(at, main), :] = x_ref[v, pl.ds(f * main, main), :].astype(F32)
            wide_ref[pl.ds(at + main, rows), :] = pltpu.roll(halo, LANES - HALO - 2 * HALO * f, 1)
    for j in range(rows):
        for t in range(tiles):
            got = wide_ref[pl.ds(t * rows + j, fields, stride=span), :]
            out_ref[j, t] = got.astype(BF16)
    send_rows(out_ref, rows - ABOVE, last_ref)
    send_rows(out_ref, 0, first_ref)
    owner = owner_ref[0]
    edges = []
    for source in ((owner + sources - 1) % sources, (owner + 1) % sources):
        parts = x_ref[source, pl.ds(2 * main, rows), :].astype(F32)
        edges.append(parts[0:1] + parts[1:2] + parts[2:3])
    edge_ref[...] = jnp.concatenate(edges, axis=0)


def regroup(x, owner):
    smem, vmem = pl.BlockSpec(memory_space=pltpu.SMEM), pl.BlockSpec(memory_space=pltpu.VMEM)
    tiles = (x.shape[1] + 8) // 16
    return pl.pallas_call(
        regroup_kernel,
        out_shape=state_shapes(8, tiles, 32) + [jax.ShapeDtypeStruct((2, LANES), F32)],
        in_specs=[smem, vmem],
        out_specs=[vmem] * 4,
        scratch_shapes=[pltpu.VMEM((32 * tiles * 8, LANES), F32)],
        compiler_params=pltpu.CompilerParams(vmem_limit_bytes=8 << 20),
        name="regroup",
    )(owner, x)


def advance_kernel(last, param_ref, edge_ref, before_ref, now_ref, after_ref, phys_ref, bias_ref, *refs):
    rows, tiles, fields = now_ref.shape[:3]
    s_ref = refs[-1]
    take_rows(before_ref, 0, s_ref)
    s_ref[pl.ds(ABOVE, rows)] = now_ref[...]
    take_rows(after_ref, ABOVE + rows, s_ref)
    bands = rows // BLOCK_ROWS
    lane = lax.broadcasted_iota(jnp.int32, (fields, LANES), 1)
    left_half = lane < LANES // 2
    phys = phys_ref[...]
    bias = jnp.broadcast_to(bias_ref[...], (LANES, fields)).T

    def departed(band, block, tile):
        if 0 <= block < 5:
            start = ((last * bands + band) * 5 + block) * PER_BLOCK
            value = [param_ref[start + k] for k in range(PER_BLOCK)]
        else:
            west = block < 0
            start = STAMP_LANE + (west * bands + band) * PER_BLOCK
            value = [edge_ref[0 if west else 1, start + k] for k in range(PER_BLOCK)]
        base = ABOVE - 2 + band * BLOCK_ROWS - value[0].astype(jnp.int32)
        first = -value[1].astype(jnp.int32) - 2
        wr, wc = value[2:6], value[6:10]
        centre, edge = [], []
        for k in range(BLOCK_ROWS + 3):
            before = s_ref[base + k, (tile + tiles - 1) % tiles].astype(F32)
            after = s_ref[base + k, (tile + 1) % tiles].astype(F32)
            centre.append(s_ref[base + k, tile].astype(F32))
            edge.append(jnp.where(left_half, after, before))
        taps = []
        for b in range(4):
            shift = first + b
            outside = (lane < shift) | (lane >= LANES + shift)
            taps.append((outside, (LANES - shift) & (LANES - 1)))
        result = []
        for i in range(BLOCK_ROWS):
            c = sum(wr[a] * centre[i + a] for a in range(4))
            e = sum(wr[a] * edge[i + a] for a in range(4))
            total = None
            for b in range(4):
                outside, turn = taps[b]
                term = wc[b] * pltpu.roll(jnp.where(outside, e, c), turn, 1)
                total = term if total is None else total + term
            result.append(total)
        return result

    for band in range(bands):
        for tile in range(5 if last else 6):
            if tile < 5:
                dep = departed(band, tile, tile)
            else:
                right = departed(band, 5, tile)
                left = departed(band, -1, tile)
                dep = [jnp.where(left_half, r, l) for r, l in zip(right, left)]
            low = jnp.concatenate(dep, axis=1).astype(BF16)
            forcing = jnp.dot(phys, low, preferred_element_type=F32)
            for i in range(BLOCK_ROWS):
                push = forcing[:, i * LANES : (i + 1) * LANES] + bias
                value = dep[i] + jnp.tanh(push)
                row = band * BLOCK_ROWS + i
                if last:
                    refs[1][pl.ds((row * 5 + tile) * fields, fields), :] = value
                else:
                    refs[0][row, tile] = value.astype(BF16)
    if not last:
        send_rows(refs[0], rows - ABOVE, refs[1])
        send_rows(refs[0], 0, refs[2])
    if last:
        for f in range(fields):
            for t in range(5):
                got = refs[1][pl.ds(t * fields + f, rows, stride=5 * fields), :]
                refs[0][f, :, pl.ds(t * LANES, LANES)] = got.astype(BF16)


def advance(last, params, edges, before, now, after, phys, bias):
    rows, tiles, fields = now.shape[:3]
    smem, vmem = pl.BlockSpec(memory_space=pltpu.SMEM), pl.BlockSpec(memory_space=pltpu.VMEM)
    scratch = [pltpu.VMEM((ABOVE + rows + BELOW, tiles, fields, LANES), BF16)]
    if last:
        shape = jax.ShapeDtypeStruct((fields, rows, 5 * LANES), BF16)
        scratch.insert(0, pltpu.VMEM((rows * 5 * fields, LANES), F32))
    else:
        shape = state_shapes(rows, tiles, fields)
    return pl.pallas_call(
        functools.partial(advance_kernel, last),
        out_shape=shape,
        in_specs=[smem] * 2 + [vmem] * 5,
        scratch_shapes=scratch,
        compiler_params=pltpu.CompilerParams(vmem_limit_bytes=16 << 20),
        name="advance_last" if last else "advance_first",
    )(params, edges, before, now, after, phys, bias)


def row_halos(last, first):
    size = lax.axis_size("wave")
    before = lax.ppermute(last, "wave", [(i, i + 1) for i in range(size - 1)])
    after = lax.ppermute(first, "wave", [(i + 1, i) for i in range(size - 1)])
    return before, after


def shards(spectral, wave_ids, lat_rows, shift_rows, shift_cols, frac_rows, frac_cols, phys_weight, phys_bias):
    slots, parts, fields, waves = spectral.shape
    lats = lat_rows.shape[0]
    bands, owners = lax.axis_size("wave"), lax.axis_size("lev")
    nlon = shift_rows.shape[2] * BLOCK_COLS * owners
    scale = 1.0 / math.sqrt(waves)
    band = lax.axis_index("wave").astype(jnp.int32).reshape(1)
    owner = lax.axis_index("lev").astype(jnp.int32).reshape(1)
    outgoing = legendre(
        spectral, wave_ids, band, lat_rows, 8 * lats, nlon // owners - 1, 2 * nlon, scale
    )
    outgoing = outgoing.reshape(bands, lats // bands, slots * parts * fields)
    arrived = lax.all_to_all(outgoing, "wave", split_axis=0, concat_axis=0, tiled=True)
    table, m, stamp, params = fourier_table(
        wave_ids[None, :], shift_rows, shift_cols, frac_rows, frac_cols, 2 * nlon, 6
    )
    bias = phys_bias[None, :]
    arrived, params, bias = lax.optimization_barrier((arrived, params, bias))
    columns = fourier(arrived, m, stamp, table, scale)
    columns = lax.all_to_all(columns, "lev", split_axis=0, concat_axis=0, tiled=True)
    state, last, first, edges = regroup(columns, owner)
    before, after = row_halos(last, first)
    state, last, first = advance(False, params, edges, before, state, after, phys_weight, bias)
    before, after = row_halos(last, first)
    return advance(True, params, edges, before, state, after, phys_weight, bias)


def solution(mesh):
    blocks = P(None, "wave", "lev")
    return jax.shard_map(
        shards,
        mesh=mesh,
        in_specs=(P("wave", None, "lev", None), P(), P(), blocks, blocks, blocks, blocks, P(), P()),
        out_specs=P(None, "wave", "lev"),
        check_vma=False,
    )
```

```python
import functools
import math

import jax
import jax.numpy as jnp
from jax import lax
from jax.experimental import pallas as pl
from jax.experimental.pallas import tpu as pltpu
from jax.sharding import PartitionSpec as P

BLOCK_ROWS = 4
BLOCK_COLS = 128
LANES = 128
ABOVE = 6
BELOW = 5
HALO = 16
STAMP_LANE = 4 * HALO
PER_BLOCK = 10
F32 = jnp.float32
BF16 = jnp.bfloat16
NT = (((1,), (1,)), ((), ()))


def sincos(x, period):
    quarter = period // 4
    turns = jnp.floor(x * (1.0 / quarter) + 0.5)
    t = (x - turns * float(quarter)) * (2.0 * math.pi / period)
    t2 = t * t
    s = t * (1.0 + t2 * (-1.0 / 6.0 + t2 * (1.0 / 120.0 + t2 * (-1.0 / 5040.0))))
    c = 1.0 + t2 * (-0.5 + t2 * (1.0 / 24.0 + t2 * (-1.0 / 720.0 + t2 * (1.0 / 40320.0))))
    k = turns.astype(jnp.int32)
    swap = (k & 1) == 1
    cos, sin = jnp.where(swap, s, c), jnp.where(swap, c, s)
    cos = jnp.where(((k + 1) & 2) != 0, -cos, cos)
    sin = jnp.where((k & 2) != 0, -sin, sin)
    return cos, sin


def rotate(c, s, rc, rs):
    return c * rc - s * rs, s * rc + c * rs


def down(row):
    return jnp.broadcast_to(row, (LANES, LANES)).T


def legendre_kernel(
    period, middle, turn, scale, ids_hbm, lat_hbm, band_ref, x_hbm, out_ref, cos_ref, sin_ref, cw_ref, sw_ref, lat_ref,
    ids_ref, lat_in_ref, x_ref, sems,
):
    loads = [
        pltpu.make_async_copy(src, dst, sems.at[i])
        for i, (src, dst) in enumerate(((ids_hbm, ids_ref), (lat_hbm, lat_in_ref), (x_hbm, x_ref)))
    ]
    for load in loads:
        load.start()
    rows, waves = 4 * x_ref.shape[0], x_ref.shape[3]
    half = waves // 2
    lats = out_ref.shape[0]
    slots = rows // 4
    step = 32
    lane = lax.broadcasted_iota(jnp.int32, (1, LANES), 1)
    first = band_ref[0] * slots
    loads[0].wait()
    m_row = jnp.zeros((1, LANES), jnp.int32)
    for s in range(slots):
        m_row = jnp.where(lane // 4 == s, ids_ref[first + s], m_row)
    m_row = m_row.astype(F32)
    loads[1].wait()
    for i in range(lats // LANES):
        row = lat_in_ref[pl.ds(i * LANES, LANES)].astype(F32).reshape(1, LANES)
        lat_ref[pl.ds(i * LANES, LANES), :] = down(row)
    odd = 2.0 * lax.broadcasted_iota(jnp.int32, (step, LANES), 1).astype(F32) + 1.0
    centre = jnp.broadcast_to(2.0 * m_row + float(waves - 1), (step, LANES))

    def fill(i, carry):
        at = pl.ds(pl.multiple_of(i * step, step), step)
        lat = lat_ref[at, :]
        cw, sw = sincos(lat * centre, 2 * period)
        cw_ref[at, :] = cw
        sw_ref[at, :] = sw
        c, s = sincos(lat * odd, 2 * period)
        rc, rs = sincos(lat * float(LANES), period)
        for a in range(half // LANES):
            cols = pl.ds(a * LANES, LANES)
            cos_ref[at, cols] = c.astype(BF16)
            sin_ref[at, cols] = s.astype(BF16)
            if a + 1 < half // LANES:
                c, s = rotate(c, s, rc, rs)
        return carry

    lax.fori_loop(0, lats // step, fill, 0)
    loads[2].wait()
    m_col = down(m_row)
    k = lax.broadcasted_iota(jnp.int32, (rows, LANES), 1).astype(F32)
    kept = []
    for a in range(waves // LANES):
        part = x_ref[:, :, :, pl.ds(a * LANES, LANES)].astype(F32).reshape(rows, LANES)
        kept.append(jnp.where(k < (waves - a * LANES) - m_col, part, 0.0).astype(BF16))
    src = lax.broadcasted_iota(jnp.int32, (rows, rows), 0)
    dst = lax.broadcasted_iota(jnp.int32, (rows, rows), 1)
    flip = jnp.where(src + dst == LANES - 1, 1.0, 0.0).astype(BF16)
    count = half // LANES
    upper = jnp.concatenate(kept[count:], axis=1)
    lower = jnp.concatenate(
        [jnp.dot(part, flip, preferred_element_type=F32).astype(BF16) for part in kept[count - 1 :: -1]], axis=1
    )
    both = jnp.concatenate([upper, lower], axis=0)
    even = lax.dot_general(cos_ref[...], both, NT, preferred_element_type=F32)
    odds = lax.dot_general(sin_ref[...], both, NT, preferred_element_type=F32)
    even = even[:, :rows] + even[:, rows:]
    odds = odds[:, :rows] - odds[:, rows:]
    leg = (cw_ref[...] * even - sw_ref[...] * odds) * scale
    cos, sin = sincos(m_row * float(middle), turn)
    real = lane % 4 < 2
    other = jnp.where(real, pltpu.roll(leg, LANES - 2, 1), pltpu.roll(leg, 2, 1))
    leg = (leg * cos + other * jnp.where(real, -sin, sin)).astype(BF16)
    order = jnp.where((src % 4) * slots + src // 4 == dst, 1.0, 0.0).astype(BF16)
    out_ref[...] = jnp.dot(leg, order, preferred_element_type=F32).astype(BF16)


def legendre(x, wave_ids, band, lat_rows, period, middle, turn, scale):
    rows, waves = 4 * x.shape[0], x.shape[3]
    lats = lat_rows.shape[0]
    hbm, smem = pl.BlockSpec(memory_space=pltpu.HBM), pl.BlockSpec(memory_space=pltpu.SMEM)
    vmem = pl.BlockSpec(memory_space=pltpu.VMEM)
    return pl.pallas_call(
        functools.partial(legendre_kernel, period, middle, turn, scale),
        out_shape=jax.ShapeDtypeStruct((lats, rows), BF16),
        in_specs=[hbm, hbm, smem, hbm],
        out_specs=vmem,
        scratch_shapes=[
            pltpu.VMEM((lats, waves // 2), BF16),
            pltpu.VMEM((lats, waves // 2), BF16),
            pltpu.VMEM((lats, LANES), F32),
            pltpu.VMEM((lats, LANES), F32),
            pltpu.VMEM((lats, LANES), F32),
            pltpu.SMEM(wave_ids.shape, jnp.int32),
            pltpu.VMEM(lat_rows.shape, jnp.int32),
            pltpu.VMEM(x.shape, BF16),
            pltpu.SemaphoreType.DMA((3,)),
        ],
        compiler_params=pltpu.CompilerParams(vmem_limit_bytes=67043328),
        name="legendre",
    )(wave_ids, lat_rows, band, x)


def times_i(z, power):
    re, im = z
    return ((re, im), (-im, re), (-re, -im), (im, -re))[power % 4]


def add(*terms):
    re, im = terms[0]
    for r, i in terms[1:]:
        re, im = re + r, im + i
    return re, im


def four(z):
    a, b = add(z[0], z[2]), add(z[0], times_i(z[2], 2))
    c, d = add(z[1], z[3]), add(z[1], times_i(z[3], 2))
    return add(a, c), add(b, times_i(d, 1)), add(a, times_i(c, 2)), add(b, times_i(d, 3))


def sixteen_real(y):
    inner = [four([y[4 * q1 + q0] for q1 in range(4)]) for q0 in range(4)]
    out = [None] * 16
    for a0 in range(4):
        v = []
        for q0 in range(4):
            re, im = inner[q0][a0]
            if q0 * a0:
                angle = 2.0 * math.pi * q0 * a0 / 16.0
                cos, sin = math.cos(angle), math.sin(angle)
                re, im = re * cos - im * sin, re * sin + im * cos
            v.append((re, im))
        even, odd = v[0][0] + v[2][0], v[0][0] - v[2][0]
        plus, minus = v[1][0] + v[3][0], v[3][1] - v[1][1]
        out[a0], out[a0 + 8] = even + plus, even - plus
        out[a0 + 4], out[a0 + 12] = odd + minus, odd - minus
    return out


def cubic_weights(fraction):
    coord = 1.0 - fraction
    return (
        -coord * (coord - 1.0) * (coord - 2.0) * (1.0 / 6.0),
        (coord + 1.0) * (coord - 1.0) * (coord - 2.0) * 0.5,
        -(coord + 1.0) * coord * (coord - 2.0) * 0.5,
        (coord + 1.0) * coord * (coord - 1.0) * (1.0 / 6.0),
    )


def table_kernel(period, ids_ref, sr_ref, sc_ref, fr_ref, fc_ref, e_ref, m_ref, stamp_ref, param_ref):
    waves = ids_ref.shape[1]
    spans = e_ref.shape[0] // LANES
    odd = 2.0 * lax.broadcasted_iota(jnp.int32, (8, LANES), 0).astype(F32) + 1.0
    m_ref[...] = ids_ref[...].astype(F32)

    def fill(i, carry):
        at = pl.ds(pl.multiple_of(i * LANES, LANES), LANES)
        m = jnp.broadcast_to(ids_ref[:, at].astype(F32), (8, LANES))
        c8, s8 = sincos(m * 16.0, period)
        c64, s64 = sincos(m * 128.0, period)
        z = [sincos(m * odd, period)]
        for _ in range(7):
            z.append(rotate(*z[-1], c8, s8))
        for t in range(spans):
            base = 256 * (t // 2) + 64 * (t % 2)
            for h in range(4):
                (c0, s0), (c1, s1) = z[2 * h], z[2 * h + 1]
                e_ref[pl.ds(base + h * 16, 16), at] = jnp.concatenate([c0, c1], axis=0).astype(BF16)
                e_ref[pl.ds(base + 128 + h * 16, 16), at] = jnp.concatenate([s0, s1], axis=0).astype(BF16)
            if t + 1 < spans:
                z = [rotate(a, b, c64, s64) for a, b in z]
        return carry

    lax.fori_loop(0, waves // LANES, fill, 0)
    steps, bands, blocks = sr_ref.shape
    lane = lax.broadcasted_iota(jnp.int32, (8, LANES), 1)
    row = lax.broadcasted_iota(jnp.int32, (8, LANES), 0)
    stamp = jnp.zeros((8, LANES), F32)
    for step in range(steps):
        for band in range(bands):
            for block in range(blocks):
                moves = (sr_ref[step, band, block].astype(F32), sc_ref[step, band, block].astype(F32))
                values = moves + cubic_weights(fr_ref[step, band, block]) + cubic_weights(fc_ref[step, band, block])
                for k, value in enumerate(values):
                    param_ref[((step * bands + band) * blocks + block) * PER_BLOCK + k] = value
                    side = {0: 0, blocks - 1: 1}.get(block)
                    if step == 0 and side is not None:
                        at = STAMP_LANE + (side * bands + band) * PER_BLOCK + k
                        stamp = jnp.where(lane == at, value, stamp)
    high = stamp.astype(BF16).astype(F32)
    mid = (stamp - high).astype(BF16).astype(F32)
    stamp_ref[...] = jnp.where(row == 0, high, jnp.where(row == 1, mid, jnp.where(row == 2, stamp - high - mid, 0.0)))


def fourier_table(ids, shift_rows, shift_cols, frac_rows, frac_cols, period, tiles):
    waves = ids.shape[1]
    smem, vmem = pl.BlockSpec(memory_space=pltpu.SMEM), pl.BlockSpec(memory_space=pltpu.VMEM)
    return pl.pallas_call(
        functools.partial(table_kernel, period),
        out_shape=[
            jax.ShapeDtypeStruct((tiles * LANES, waves), BF16),
            jax.ShapeDtypeStruct((1, waves), F32),
            jax.ShapeDtypeStruct((8, LANES), F32),
            jax.ShapeDtypeStruct((shift_rows.size * PER_BLOCK,), F32),
        ],
        in_specs=[vmem] + [smem] * 4,
        out_specs=[vmem, vmem, vmem, smem],
        compiler_params=pltpu.CompilerParams(vmem_limit_bytes=8 << 20),
        cost_estimate=pl.CostEstimate(flops=20000000, bytes_accessed=2500000, transcendentals=0),
        name="fourier_table",
    )(ids, shift_rows, shift_cols, frac_rows, frac_cols)


def fourier_kernel(scale, z_ref, m_ref, stamp_ref, e_ref, out_ref, l_ref, d_ref, g_ref):
    waves = m_ref.shape[1]
    group = lax.broadcasted_iota(jnp.int32, (8, LANES), 1) // 32

    def spread(i, carry):
        at = pl.ds(pl.multiple_of(i * LANES, LANES), LANES)
        block = [z_ref[4 * i + u].astype(F32) for u in range(4)]
        parts = []
        for cf in range(4):
            whole = None
            for u in range(4):
                turn = (32 * (u - cf)) % LANES
                moved = pltpu.roll(block[u], turn, 1) if turn else block[u]
                whole = moved if whole is None else jnp.where(group == u, moved, whole)
            parts.append(whole)
        both = jnp.concatenate(parts, axis=0)
        m = jnp.broadcast_to(m_ref[:, at], both.shape)
        residue = m - 16.0 * jnp.floor(m * 0.0625)
        for q in range(16):
            l_ref[pl.ds(q * 32, 32), at] = jnp.where(residue == float(q), both, 0.0).astype(BF16)
        return carry

    lax.fori_loop(0, waves // LANES, spread, 0)
    halves = e_ref.shape[0] // 256
    low, high = pl.ds(0, LANES), pl.ds(LANES, LANES)
    for p in range(halves):
        d_ref[...] = lax.dot_general(l_ref[...], e_ref[pl.ds(p * 256, 256), :], NT, preferred_element_type=F32)
        right, left = [], []
        for q in range(16):
            re, im = pl.ds(q * 32, 16), pl.ds(q * 32 + 16, 16)
            c0, c1, s0, s1 = d_ref[re, low], d_ref[im, low], d_ref[re, high], d_ref[im, high]
            right.append((c0 - s1, c1 + s0))
            left.append((c0 + s1, c1 - s0))
        for side, y in ((halves + p, right), (halves - 1 - p, left)):
            for a, value in enumerate(sixteen_real(y)):
                g_ref[side, pl.ds(a * 16, 16), :] = (value * scale).astype(BF16)

    src = lax.broadcasted_iota(jnp.int32, (LANES, LANES), 0)
    dst = lax.broadcasted_iota(jnp.int32, (LANES, LANES), 1)
    half = LANES // 2

    def pick(mirrored, upper):
        want = (half - 1 + LANES * upper - dst) if mirrored else (dst + half - LANES * upper)
        inside = (dst >= half) if upper else (dst < half)
        return jnp.where(inside & (src == want), 1.0, 0.0).astype(BF16)

    lane = lax.broadcasted_iota(jnp.int32, (8, LANES), 1)
    stamp = stamp_ref[...]
    tiles = 2 * halves
    for t in range(tiles):
        first, second = t, (t + 1) % tiles
        value = jnp.dot(g_ref[first], pick(first < halves, 0), preferred_element_type=F32) + jnp.dot(
            g_ref[second], pick(second < halves, 1), preferred_element_type=F32
        )
        for a in range(16):
            one, two = value[a * 16 : a * 16 + 8], value[a * 16 + 8 : a * 16 + 16]
            if t < tiles - 1:
                out_ref[a, pl.ds(t * 8, 8), :] = one.astype(BF16)
                out_ref[a, pl.ds((tiles - 1 + t) * 8, 8), :] = two.astype(BF16)
            else:
                one, two = pltpu.roll(one, HALO, 1), pltpu.roll(two, 3 * HALO, 1)
                halo = jnp.where(lane < 2 * HALO, one, jnp.where(lane < STAMP_LANE, two, stamp))
                out_ref[a, pl.ds((tiles - 1) * 16, 8), :] = halo.astype(BF16)


def fourier(z, m, stamp, table, scale):
    tiles = table.shape[0] // LANES
    vmem = pl.BlockSpec(memory_space=pltpu.VMEM)
    return pl.pallas_call(
        functools.partial(fourier_kernel, scale),
        out_shape=jax.ShapeDtypeStruct((16, tiles * 16 - 8, LANES), BF16),
        in_specs=[vmem] * 4,
        out_specs=vmem,
        scratch_shapes=[
            pltpu.VMEM((512, table.shape[1]), BF16),
            pltpu.VMEM((512, 256), F32),
            pltpu.VMEM((tiles, 256, LANES), BF16),
        ],
        compiler_params=pltpu.CompilerParams(vmem_limit_bytes=24 << 20),
        name="fourier",
    )(z, m, stamp, table)


def send_rows(state_ref, first, sent_ref):
    fields = state_ref.shape[2]
    lane = lax.broadcasted_iota(jnp.int32, (8, LANES), 1)
    for r in range(sent_ref.shape[0]):
        for t in range(5):
            sent_ref[r, pl.ds(t * fields, fields)] = state_ref[first + r, t]
        halo = state_ref[first + r, 5].astype(F32)
        packed = pltpu.roll(halo[0:8], HALO, 1)
        for g in range(1, fields // 8):
            packed = jnp.where(lane < 2 * HALO * g, packed, pltpu.roll(halo[8 * g : 8 * g + 8], HALO * (2 * g + 1), 1))
        sent_ref[r, pl.ds(5 * fields, 8)] = packed.astype(BF16)


def take_rows(got_ref, first, state_ref):
    fields = state_ref.shape[2]
    for r in range(got_ref.shape[0]):
        for t in range(5):
            state_ref[first + r, t] = got_ref[r, pl.ds(t * fields, fields)]
        packed = got_ref[r, pl.ds(5 * fields, 8)].astype(F32)
        halo = [pltpu.roll(packed, (LANES - HALO * (2 * g + 1)) % LANES, 1) for g in range(fields // 8)]
        state_ref[first + r, 5] = jnp.concatenate(halo, axis=0).astype(BF16)


def state_shapes(rows, tiles, fields):
    shapes = [(rows, tiles, fields, LANES)] + [(n, 5 * fields + 8, LANES) for n in (ABOVE, BELOW)]
    return [jax.ShapeDtypeStruct(shape, BF16) for shape in shapes]


def regroup_kernel(owner_ref, x_ref, out_ref, last_ref, first_ref, edge_ref, wide_ref):
    rows, tiles, fields = out_ref.shape[:3]
    sources = x_ref.shape[0]
    main, span = (tiles - 1) * rows, tiles * rows
    for v in range(sources):
        halo = x_ref[v, pl.ds(2 * main, rows), :].astype(F32)
        for f in range(2):
            at = (2 * v + f) * span
            wide_ref[pl.ds(at, main), :] = x_ref[v, pl.ds(f * main, main), :].astype(F32)
            wide_ref[pl.ds(at + main, rows), :] = pltpu.roll(halo, LANES - HALO - 2 * HALO * f, 1)
    for j in range(rows):
        for t in range(tiles):
            got = wide_ref[pl.ds(t * rows + j, fields, stride=span), :]
            out_ref[j, t] = got.astype(BF16)
    send_rows(out_ref, rows - ABOVE, last_ref)
    send_rows(out_ref, 0, first_ref)
    owner = owner_ref[0]
    edges = []
    for source in ((owner + sources - 1) % sources, (owner + 1) % sources):
        parts = x_ref[source, pl.ds(2 * main, rows), :].astype(F32)
        edges.append(parts[0:1] + parts[1:2] + parts[2:3])
    edge_ref[...] = jnp.concatenate(edges, axis=0)


def regroup(x, owner):
    smem, vmem = pl.BlockSpec(memory_space=pltpu.SMEM), pl.BlockSpec(memory_space=pltpu.VMEM)
    tiles = (x.shape[1] + 8) // 16
    return pl.pallas_call(
        regroup_kernel,
        out_shape=state_shapes(8, tiles, 32) + [jax.ShapeDtypeStruct((2, LANES), F32)],
        in_specs=[smem, vmem],
        out_specs=[vmem] * 4,
        scratch_shapes=[pltpu.VMEM((32 * tiles * 8, LANES), F32)],
        compiler_params=pltpu.CompilerParams(vmem_limit_bytes=8 << 20),
        name="regroup",
    )(owner, x)


def advance_kernel(last, param_ref, edge_ref, before_ref, now_ref, after_ref, phys_ref, bias_ref, *refs):
    rows, tiles, fields = now_ref.shape[:3]
    s_ref = refs[-1]
    take_rows(before_ref, 0, s_ref)
    s_ref[pl.ds(ABOVE, rows)] = now_ref[...]
    take_rows(after_ref, ABOVE + rows, s_ref)
    bands = rows // BLOCK_ROWS
    lane = lax.broadcasted_iota(jnp.int32, (fields, LANES), 1)
    left_half = lane < LANES // 2
    phys = phys_ref[...]
    bias = jnp.broadcast_to(bias_ref[...], (LANES, fields)).T

    def departed(band, block, tile):
        if 0 <= block < 5:
            start = ((last * bands + band) * 5 + block) * PER_BLOCK
            value = [param_ref[start + k] for k in range(PER_BLOCK)]
        else:
            west = block < 0
            start = STAMP_LANE + (west * bands + band) * PER_BLOCK
            value = [edge_ref[0 if west else 1, start + k] for k in range(PER_BLOCK)]
        base = ABOVE - 2 + band * BLOCK_ROWS - value[0].astype(jnp.int32)
        first = -value[1].astype(jnp.int32) - 2
        wr, wc = value[2:6], value[6:10]
        centre, edge = [], []
        for k in range(BLOCK_ROWS + 3):
            before = s_ref[base + k, (tile + tiles - 1) % tiles].astype(F32)
            after = s_ref[base + k, (tile + 1) % tiles].astype(F32)
            centre.append(s_ref[base + k, tile].astype(F32))
            edge.append(jnp.where(left_half, after, before))
        taps = []
        for b in range(4):
            shift = first + b
            outside = (lane < shift) | (lane >= LANES + shift)
            taps.append((outside, (LANES - shift) & (LANES - 1)))
        result = []
        for i in range(BLOCK_ROWS):
            c = sum(wr[a] * centre[i + a] for a in range(4))
            e = sum(wr[a] * edge[i + a] for a in range(4))
            total = None
            for b in range(4):
                outside, turn = taps[b]
                term = wc[b] * pltpu.roll(jnp.where(outside, e, c), turn, 1)
                total = term if total is None else total + term
            result.append(total)
        return result

    for band in range(bands):
        for tile in range(5 if last else 6):
            if tile < 5:
                dep = departed(band, tile, tile)
            else:
                right = departed(band, 5, tile)
                left = departed(band, -1, tile)
                dep = [jnp.where(left_half, r, l) for r, l in zip(right, left)]
            low = jnp.concatenate(dep, axis=1).astype(BF16)
            forcing = jnp.dot(phys, low, preferred_element_type=F32)
            for i in range(BLOCK_ROWS):
                push = forcing[:, i * LANES : (i + 1) * LANES] + bias
                value = dep[i] + jnp.tanh(push)
                row = band * BLOCK_ROWS + i
                if last:
                    refs[1][pl.ds((row * 5 + tile) * fields, fields), :] = value
                else:
                    refs[0][row, tile] = value.astype(BF16)
    if not last:
        send_rows(refs[0], rows - ABOVE, refs[1])
        send_rows(refs[0], 0, refs[2])
    if last:
        for f in range(fields):
            for t in range(5):
                got = refs[1][pl.ds(t * fields + f, rows, stride=5 * fields), :]
                refs[0][f, :, pl.ds(t * LANES, LANES)] = got.astype(BF16)


def advance(last, params, edges, before, now, after, phys, bias):
    rows, tiles, fields = now.shape[:3]
    smem, vmem = pl.BlockSpec(memory_space=pltpu.SMEM), pl.BlockSpec(memory_space=pltpu.VMEM)
    scratch = [pltpu.VMEM((ABOVE + rows + BELOW, tiles, fields, LANES), BF16)]
    if last:
        shape = jax.ShapeDtypeStruct((fields, rows, 5 * LANES), BF16)
        scratch.insert(0, pltpu.VMEM((rows * 5 * fields, LANES), F32))
    else:
        shape = state_shapes(rows, tiles, fields)
    return pl.pallas_call(
        functools.partial(advance_kernel, last),
        out_shape=shape,
        in_specs=[smem] * 2 + [vmem] * 5,
        scratch_shapes=scratch,
        compiler_params=pltpu.CompilerParams(vmem_limit_bytes=16 << 20),
        name="advance_last" if last else "advance_first",
    )(params, edges, before, now, after, phys, bias)


def row_halos(last, first):
    size = lax.axis_size("wave")
    before = lax.ppermute(last, "wave", [(i, i + 1) for i in range(size - 1)])
    after = lax.ppermute(first, "wave", [(i + 1, i) for i in range(size - 1)])
    return before, after


def shards(spectral, wave_ids, lat_rows, shift_rows, shift_cols, frac_rows, frac_cols, phys_weight, phys_bias):
    slots, parts, fields, waves = spectral.shape
    lats = lat_rows.shape[0]
    bands, owners = lax.axis_size("wave"), lax.axis_size("lev")
    nlon = shift_rows.shape[2] * BLOCK_COLS * owners
    scale = 1.0 / math.sqrt(waves)
    band = lax.axis_index("wave").astype(jnp.int32).reshape(1)
    owner = lax.axis_index("lev").astype(jnp.int32).reshape(1)
    outgoing = legendre(
        spectral, wave_ids, band, lat_rows, 8 * lats, nlon // owners - 1, 2 * nlon, scale
    )
    outgoing = outgoing.reshape(bands, lats // bands, slots * parts * fields)
    arrived = lax.all_to_all(outgoing, "wave", split_axis=0, concat_axis=0, tiled=True)
    table, m, stamp, params = fourier_table(
        wave_ids[None, :], shift_rows, shift_cols, frac_rows, frac_cols, 2 * nlon, 6
    )
    bias = phys_bias[None, :]
    arrived, params, bias, owner = lax.optimization_barrier((arrived, params, bias, owner))
    columns = fourier(arrived, m, stamp, table, scale)
    columns = lax.all_to_all(columns, "lev", split_axis=0, concat_axis=0, tiled=True)
    state, last, first, edges = regroup(columns, owner)
    before, after = row_halos(last, first)
    state, last, first = advance(False, params, edges, before, state, after, phys_weight, bias)
    before, after = row_halos(last, first)
    return advance(True, params, edges, before, state, after, phys_weight, bias)


def solution(mesh):
    blocks = P(None, "wave", "lev")
    return jax.shard_map(
        shards,
        mesh=mesh,
        in_specs=(P("wave", None, "lev", None), P(), P(), blocks, blocks, blocks, blocks, P(), P()),
        out_specs=P(None, "wave", "lev"),
        check_vma=False,
    )
```

```python
import functools
import math

import jax
import jax.numpy as jnp
from jax import lax
from jax.experimental import pallas as pl
from jax.experimental.pallas import tpu as pltpu
from jax.sharding import PartitionSpec as P

BLOCK_ROWS = 4
BLOCK_COLS = 128
LANES = 128
ABOVE = 6
BELOW = 5
HALO = 16
STAMP_LANE = 4 * HALO
PER_BLOCK = 10
F32 = jnp.float32
BF16 = jnp.bfloat16
NT = (((1,), (1,)), ((), ()))


def sincos(x, period):
    quarter = period // 4
    turns = jnp.floor(x * (1.0 / quarter) + 0.5)
    t = (x - turns * float(quarter)) * (2.0 * math.pi / period)
    t2 = t * t
    s = t * (1.0 + t2 * (-1.0 / 6.0 + t2 * (1.0 / 120.0 + t2 * (-1.0 / 5040.0))))
    c = 1.0 + t2 * (-0.5 + t2 * (1.0 / 24.0 + t2 * (-1.0 / 720.0 + t2 * (1.0 / 40320.0))))
    k = turns.astype(jnp.int32)
    swap = (k & 1) == 1
    cos, sin = jnp.where(swap, s, c), jnp.where(swap, c, s)
    cos = jnp.where(((k + 1) & 2) != 0, -cos, cos)
    sin = jnp.where((k & 2) != 0, -sin, sin)
    return cos, sin


def rotate(c, s, rc, rs):
    return c * rc - s * rs, s * rc + c * rs


def position(axis):
    return lax.axis_index(axis)


def down(row):
    return jnp.broadcast_to(row, (LANES, LANES)).T


def legendre_kernel(
    period, middle, turn, scale, ids_hbm, lat_hbm, x_hbm, out_ref, cos_ref, sin_ref, cw_ref, sw_ref, lat_ref,
    ids_ref, lat_in_ref, x_ref, sems,
):
    loads = [
        pltpu.make_async_copy(src, dst, sems.at[i])
        for i, (src, dst) in enumerate(((ids_hbm, ids_ref), (lat_hbm, lat_in_ref), (x_hbm, x_ref)))
    ]
    for load in loads:
        load.start()
    rows, waves = 4 * x_ref.shape[0], x_ref.shape[3]
    half = waves // 2
    lats = out_ref.shape[0]
    slots = rows // 4
    step = 32
    lane = lax.broadcasted_iota(jnp.int32, (1, LANES), 1)
    first = position("wave") * slots
    loads[0].wait()
    m_row = jnp.zeros((1, LANES), jnp.int32)
    for s in range(slots):
        m_row = jnp.where(lane // 4 == s, ids_ref[first + s], m_row)
    m_row = m_row.astype(F32)
    loads[1].wait()
    for i in range(lats // LANES):
        row = lat_in_ref[pl.ds(i * LANES, LANES)].astype(F32).reshape(1, LANES)
        lat_ref[pl.ds(i * LANES, LANES), :] = down(row)
    odd = 2.0 * lax.broadcasted_iota(jnp.int32, (step, LANES), 1).astype(F32) + 1.0
    centre = jnp.broadcast_to(2.0 * m_row + float(waves - 1), (step, LANES))

    def fill(i, carry):
        at = pl.ds(pl.multiple_of(i * step, step), step)
        lat = lat_ref[at, :]
        cw, sw = sincos(lat * centre, 2 * period)
        cw_ref[at, :] = cw
        sw_ref[at, :] = sw
        c, s = sincos(lat * odd, 2 * period)
        rc, rs = sincos(lat * float(LANES), period)
        for a in range(half // LANES):
            cols = pl.ds(a * LANES, LANES)
            cos_ref[at, cols] = c.astype(BF16)
            sin_ref[at, cols] = s.astype(BF16)
            if a + 1 < half // LANES:
                c, s = rotate(c, s, rc, rs)
        return carry

    lax.fori_loop(0, lats // step, fill, 0)
    loads[2].wait()
    m_col = down(m_row)
    k = lax.broadcasted_iota(jnp.int32, (rows, LANES), 1).astype(F32)
    kept = []
    for a in range(waves // LANES):
        part = x_ref[:, :, :, pl.ds(a * LANES, LANES)].astype(F32).reshape(rows, LANES)
        kept.append(jnp.where(k < (waves - a * LANES) - m_col, part, 0.0).astype(BF16))
    src = lax.broadcasted_iota(jnp.int32, (rows, rows), 0)
    dst = lax.broadcasted_iota(jnp.int32, (rows, rows), 1)
    flip = jnp.where(src + dst == LANES - 1, 1.0, 0.0).astype(BF16)
    count = half // LANES
    upper = jnp.concatenate(kept[count:], axis=1)
    lower = jnp.concatenate(
        [jnp.dot(part, flip, preferred_element_type=F32).astype(BF16) for part in kept[count - 1 :: -1]], axis=1
    )
    both = jnp.concatenate([upper, lower], axis=0)
    even = lax.dot_general(cos_ref[...], both, NT, preferred_element_type=F32)
    odds = lax.dot_general(sin_ref[...], both, NT, preferred_element_type=F32)
    even = even[:, :rows] + even[:, rows:]
    odds = odds[:, :rows] - odds[:, rows:]
    leg = (cw_ref[...] * even - sw_ref[...] * odds) * scale
    cos, sin = sincos(m_row * float(middle), turn)
    real = lane % 4 < 2
    other = jnp.where(real, pltpu.roll(leg, LANES - 2, 1), pltpu.roll(leg, 2, 1))
    leg = (leg * cos + other * jnp.where(real, -sin, sin)).astype(BF16)
    order = jnp.where((src % 4) * slots + src // 4 == dst, 1.0, 0.0).astype(BF16)
    out_ref[...] = jnp.dot(leg, order, preferred_element_type=F32).astype(BF16)


def legendre(x, wave_ids, lat_rows, period, middle, turn, scale):
    rows, waves = 4 * x.shape[0], x.shape[3]
    lats = lat_rows.shape[0]
    hbm = pl.BlockSpec(memory_space=pltpu.HBM)
    vmem = pl.BlockSpec(memory_space=pltpu.VMEM)
    return pl.pallas_call(
        functools.partial(legendre_kernel, period, middle, turn, scale),
        out_shape=jax.ShapeDtypeStruct((lats, rows), BF16),
        in_specs=[hbm, hbm, hbm],
        out_specs=vmem,
        scratch_shapes=[
            pltpu.VMEM((lats, waves // 2), BF16),
            pltpu.VMEM((lats, waves // 2), BF16),
            pltpu.VMEM((lats, LANES), F32),
            pltpu.VMEM((lats, LANES), F32),
            pltpu.VMEM((lats, LANES), F32),
            pltpu.SMEM(wave_ids.shape, jnp.int32),
            pltpu.VMEM(lat_rows.shape, jnp.int32),
            pltpu.VMEM(x.shape, BF16),
            pltpu.SemaphoreType.DMA((3,)),
        ],
        compiler_params=pltpu.CompilerParams(vmem_limit_bytes=67043328),
        name="legendre",
    )(wave_ids, lat_rows, x)


def times_i(z, power):
    re, im = z
    return ((re, im), (-im, re), (-re, -im), (im, -re))[power % 4]


def add(*terms):
    re, im = terms[0]
    for r, i in terms[1:]:
        re, im = re + r, im + i
    return re, im


def four(z):
    a, b = add(z[0], z[2]), add(z[0], times_i(z[2], 2))
    c, d = add(z[1], z[3]), add(z[1], times_i(z[3], 2))
    return add(a, c), add(b, times_i(d, 1)), add(a, times_i(c, 2)), add(b, times_i(d, 3))


def sixteen_real(y):
    inner = [four([y[4 * q1 + q0] for q1 in range(4)]) for q0 in range(4)]
    out = [None] * 16
    for a0 in range(4):
        v = []
        for q0 in range(4):
            re, im = inner[q0][a0]
            if q0 * a0:
                angle = 2.0 * math.pi * q0 * a0 / 16.0
                cos, sin = math.cos(angle), math.sin(angle)
                re, im = re * cos - im * sin, re * sin + im * cos
            v.append((re, im))
        even, odd = v[0][0] + v[2][0], v[0][0] - v[2][0]
        plus, minus = v[1][0] + v[3][0], v[3][1] - v[1][1]
        out[a0], out[a0 + 8] = even + plus, even - plus
        out[a0 + 4], out[a0 + 12] = odd + minus, odd - minus
    return out


def cubic_weights(fraction):
    coord = 1.0 - fraction
    return (
        -coord * (coord - 1.0) * (coord - 2.0) * (1.0 / 6.0),
        (coord + 1.0) * (coord - 1.0) * (coord - 2.0) * 0.5,
        -(coord + 1.0) * coord * (coord - 2.0) * 0.5,
        (coord + 1.0) * coord * (coord - 1.0) * (1.0 / 6.0),
    )


def table_kernel(period, ids_ref, sr_ref, sc_ref, fr_ref, fc_ref, e_ref, m_ref, stamp_ref, param_ref):
    waves = ids_ref.shape[1]
    spans = e_ref.shape[0] // LANES
    odd = 2.0 * lax.broadcasted_iota(jnp.int32, (8, LANES), 0).astype(F32) + 1.0
    m_ref[...] = ids_ref[...].astype(F32)

    def fill(i, carry):
        at = pl.ds(pl.multiple_of(i * LANES, LANES), LANES)
        m = jnp.broadcast_to(ids_ref[:, at].astype(F32), (8, LANES))
        c8, s8 = sincos(m * 16.0, period)
        c64, s64 = sincos(m * 128.0, period)
        z = [sincos(m * odd, period)]
        for _ in range(7):
            z.append(rotate(*z[-1], c8, s8))
        for t in range(spans):
            base = 256 * (t // 2) + 64 * (t % 2)
            for h in range(4):
                (c0, s0), (c1, s1) = z[2 * h], z[2 * h + 1]
                e_ref[pl.ds(base + h * 16, 16), at] = jnp.concatenate([c0, c1], axis=0).astype(BF16)
                e_ref[pl.ds(base + 128 + h * 16, 16), at] = jnp.concatenate([s0, s1], axis=0).astype(BF16)
            if t + 1 < spans:
                z = [rotate(a, b, c64, s64) for a, b in z]
        return carry

    lax.fori_loop(0, waves // LANES, fill, 0)
    steps, bands, blocks = sr_ref.shape
    lane = lax.broadcasted_iota(jnp.int32, (8, LANES), 1)
    row = lax.broadcasted_iota(jnp.int32, (8, LANES), 0)
    stamp = jnp.zeros((8, LANES), F32)
    for step in range(steps):
        for band in range(bands):
            for block in range(blocks):
                moves = (sr_ref[step, band, block].astype(F32), sc_ref[step, band, block].astype(F32))
                values = moves + cubic_weights(fr_ref[step, band, block]) + cubic_weights(fc_ref[step, band, block])
                for k, value in enumerate(values):
                    param_ref[((step * bands + band) * blocks + block) * PER_BLOCK + k] = value
                    side = {0: 0, blocks - 1: 1}.get(block)
                    if step == 0 and side is not None:
                        at = STAMP_LANE + (side * bands + band) * PER_BLOCK + k
                        stamp = jnp.where(lane == at, value, stamp)
    high = stamp.astype(BF16).astype(F32)
    mid = (stamp - high).astype(BF16).astype(F32)
    stamp_ref[...] = jnp.where(row == 0, high, jnp.where(row == 1, mid, jnp.where(row == 2, stamp - high - mid, 0.0)))


def fourier_table(ids, shift_rows, shift_cols, frac_rows, frac_cols, period, tiles):
    waves = ids.shape[1]
    smem, vmem = pl.BlockSpec(memory_space=pltpu.SMEM), pl.BlockSpec(memory_space=pltpu.VMEM)
    return pl.pallas_call(
        functools.partial(table_kernel, period),
        out_shape=[
            jax.ShapeDtypeStruct((tiles * LANES, waves), BF16),
            jax.ShapeDtypeStruct((1, waves), F32),
            jax.ShapeDtypeStruct((8, LANES), F32),
            jax.ShapeDtypeStruct((shift_rows.size * PER_BLOCK,), F32),
        ],
        in_specs=[vmem] + [smem] * 4,
        out_specs=[vmem, vmem, vmem, smem],
        compiler_params=pltpu.CompilerParams(vmem_limit_bytes=8 << 20),
        cost_estimate=pl.CostEstimate(flops=20000000, bytes_accessed=2500000, transcendentals=0),
        name="fourier_table",
    )(ids, shift_rows, shift_cols, frac_rows, frac_cols)


def fourier_kernel(scale, z_ref, m_ref, stamp_ref, e_ref, out_ref, l_ref, d_ref, g_ref):
    waves = m_ref.shape[1]
    group = lax.broadcasted_iota(jnp.int32, (8, LANES), 1) // 32

    def spread(i, carry):
        at = pl.ds(pl.multiple_of(i * LANES, LANES), LANES)
        block = [z_ref[4 * i + u].astype(F32) for u in range(4)]
        parts = []
        for cf in range(4):
            whole = None
            for u in range(4):
                turn = (32 * (u - cf)) % LANES
                moved = pltpu.roll(block[u], turn, 1) if turn else block[u]
                whole = moved if whole is None else jnp.where(group == u, moved, whole)
            parts.append(whole)
        both = jnp.concatenate(parts, axis=0)
        m = jnp.broadcast_to(m_ref[:, at], both.shape)
        residue = m - 16.0 * jnp.floor(m * 0.0625)
        for q in range(16):
            l_ref[pl.ds(q * 32, 32), at] = jnp.where(residue == float(q), both, 0.0).astype(BF16)
        return carry

    lax.fori_loop(0, waves // LANES, spread, 0)
    halves = e_ref.shape[0] // 256
    low, high = pl.ds(0, LANES), pl.ds(LANES, LANES)
    for p in range(halves):
        d_ref[...] = lax.dot_general(l_ref[...], e_ref[pl.ds(p * 256, 256), :], NT, preferred_element_type=F32)
        right, left = [], []
        for q in range(16):
            re, im = pl.ds(q * 32, 16), pl.ds(q * 32 + 16, 16)
            c0, c1, s0, s1 = d_ref[re, low], d_ref[im, low], d_ref[re, high], d_ref[im, high]
            right.append((c0 - s1, c1 + s0))
            left.append((c0 + s1, c1 - s0))
        for side, y in ((halves + p, right), (halves - 1 - p, left)):
            for a, value in enumerate(sixteen_real(y)):
                g_ref[side, pl.ds(a * 16, 16), :] = (value * scale).astype(BF16)

    src = lax.broadcasted_iota(jnp.int32, (LANES, LANES), 0)
    dst = lax.broadcasted_iota(jnp.int32, (LANES, LANES), 1)
    half = LANES // 2

    def pick(mirrored, upper):
        want = (half - 1 + LANES * upper - dst) if mirrored else (dst + half - LANES * upper)
        inside = (dst >= half) if upper else (dst < half)
        return jnp.where(inside & (src == want), 1.0, 0.0).astype(BF16)

    lane = lax.broadcasted_iota(jnp.int32, (8, LANES), 1)
    stamp = stamp_ref[...]
    tiles = 2 * halves
    for t in range(tiles):
        first, second = t, (t + 1) % tiles
        value = jnp.dot(g_ref[first], pick(first < halves, 0), preferred_element_type=F32) + jnp.dot(
            g_ref[second], pick(second < halves, 1), preferred_element_type=F32
        )
        for a in range(16):
            one, two = value[a * 16 : a * 16 + 8], value[a * 16 + 8 : a * 16 + 16]
            if t < tiles - 1:
                out_ref[a, pl.ds(t * 8, 8), :] = one.astype(BF16)
                out_ref[a, pl.ds((tiles - 1 + t) * 8, 8), :] = two.astype(BF16)
            else:
                one, two = pltpu.roll(one, HALO, 1), pltpu.roll(two, 3 * HALO, 1)
                halo = jnp.where(lane < 2 * HALO, one, jnp.where(lane < STAMP_LANE, two, stamp))
                out_ref[a, pl.ds((tiles - 1) * 16, 8), :] = halo.astype(BF16)


def fourier(z, m, stamp, table, scale):
    tiles = table.shape[0] // LANES
    vmem = pl.BlockSpec(memory_space=pltpu.VMEM)
    return pl.pallas_call(
        functools.partial(fourier_kernel, scale),
        out_shape=jax.ShapeDtypeStruct((16, tiles * 16 - 8, LANES), BF16),
        in_specs=[vmem] * 4,
        out_specs=vmem,
        scratch_shapes=[
            pltpu.VMEM((512, table.shape[1]), BF16),
            pltpu.VMEM((512, 256), F32),
            pltpu.VMEM((tiles, 256, LANES), BF16),
        ],
        compiler_params=pltpu.CompilerParams(vmem_limit_bytes=24 << 20),
        name="fourier",
    )(z, m, stamp, table)


def send_rows(state_ref, first, sent_ref):
    fields = state_ref.shape[2]
    lane = lax.broadcasted_iota(jnp.int32, (8, LANES), 1)
    for r in range(sent_ref.shape[0]):
        for t in range(5):
            sent_ref[r, pl.ds(t * fields, fields)] = state_ref[first + r, t]
        halo = state_ref[first + r, 5].astype(F32)
        packed = pltpu.roll(halo[0:8], HALO, 1)
        for g in range(1, fields // 8):
            packed = jnp.where(lane < 2 * HALO * g, packed, pltpu.roll(halo[8 * g : 8 * g + 8], HALO * (2 * g + 1), 1))
        sent_ref[r, pl.ds(5 * fields, 8)] = packed.astype(BF16)


def take_rows(got_ref, first, state_ref):
    fields = state_ref.shape[2]
    for r in range(got_ref.shape[0]):
        for t in range(5):
            state_ref[first + r, t] = got_ref[r, pl.ds(t * fields, fields)]
        packed = got_ref[r, pl.ds(5 * fields, 8)].astype(F32)
        halo = [pltpu.roll(packed, (LANES - HALO * (2 * g + 1)) % LANES, 1) for g in range(fields // 8)]
        state_ref[first + r, 5] = jnp.concatenate(halo, axis=0).astype(BF16)


def state_shapes(rows, tiles, fields):
    shapes = [(rows, tiles, fields, LANES)] + [(n, 5 * fields + 8, LANES) for n in (ABOVE, BELOW)]
    return [jax.ShapeDtypeStruct(shape, BF16) for shape in shapes]


def regroup_kernel(x_ref, out_ref, last_ref, first_ref, edge_ref, wide_ref):
    rows, tiles, fields = out_ref.shape[:3]
    sources = x_ref.shape[0]
    main, span = (tiles - 1) * rows, tiles * rows
    for v in range(sources):
        halo = x_ref[v, pl.ds(2 * main, rows), :].astype(F32)
        for f in range(2):
            at = (2 * v + f) * span
            wide_ref[pl.ds(at, main), :] = x_ref[v, pl.ds(f * main, main), :].astype(F32)
            wide_ref[pl.ds(at + main, rows), :] = pltpu.roll(halo, LANES - HALO - 2 * HALO * f, 1)
    for j in range(rows):
        for t in range(tiles):
            got = wide_ref[pl.ds(t * rows + j, fields, stride=span), :]
            out_ref[j, t] = got.astype(BF16)
    send_rows(out_ref, rows - ABOVE, last_ref)
    send_rows(out_ref, 0, first_ref)
    owner = position("lev")
    edges = []
    for source in ((owner + sources - 1) % sources, (owner + 1) % sources):
        parts = x_ref[source, pl.ds(2 * main, rows), :].astype(F32)
        edges.append(parts[0:1] + parts[1:2] + parts[2:3])
    edge_ref[...] = jnp.concatenate(edges, axis=0)


def regroup(x):
    vmem = pl.BlockSpec(memory_space=pltpu.VMEM)
    tiles = (x.shape[1] + 8) // 16
    return pl.pallas_call(
        regroup_kernel,
        out_shape=state_shapes(8, tiles, 32) + [jax.ShapeDtypeStruct((2, LANES), F32)],
        in_specs=[vmem],
        out_specs=[vmem] * 4,
        scratch_shapes=[pltpu.VMEM((32 * tiles * 8, LANES), F32)],
        compiler_params=pltpu.CompilerParams(vmem_limit_bytes=8 << 20),
        name="regroup",
    )(x)


def advance_kernel(last, param_hbm, before_ref, now_ref, after_ref, phys_ref, bias_ref, *refs):
    rows, tiles, fields = now_ref.shape[:3]
    if not last:
        edge_hbm, *refs = refs
    *refs, s_ref, param_ref, edge_ref, sems = refs
    loads = [pltpu.make_async_copy(param_hbm, param_ref, sems.at[0])]
    if not last:
        loads.append(pltpu.make_async_copy(edge_hbm, edge_ref, sems.at[1]))
    for load in loads:
        load.start()
    take_rows(before_ref, 0, s_ref)
    s_ref[pl.ds(ABOVE, rows)] = now_ref[...]
    take_rows(after_ref, ABOVE + rows, s_ref)
    bands = rows // BLOCK_ROWS
    lane = lax.broadcasted_iota(jnp.int32, (fields, LANES), 1)
    left_half = lane < LANES // 2
    for load in loads:
        load.wait()
    phys = phys_ref[...]
    bias = jnp.broadcast_to(bias_ref[...], (LANES, fields)).T

    def departed(band, block, tile):
        if 0 <= block < 5:
            start = ((last * bands + band) * 5 + block) * PER_BLOCK
            value = [param_ref[start + k] for k in range(PER_BLOCK)]
        else:
            west = block < 0
            start = STAMP_LANE + (west * bands + band) * PER_BLOCK
            value = [edge_ref[0 if west else 1, start + k] for k in range(PER_BLOCK)]
        base = ABOVE - 2 + band * BLOCK_ROWS - value[0].astype(jnp.int32)
        first = -value[1].astype(jnp.int32) - 2
        wr, wc = value[2:6], value[6:10]
        centre, edge = [], []
        for k in range(BLOCK_ROWS + 3):
            before = s_ref[base + k, (tile + tiles - 1) % tiles]
            after = s_ref[base + k, (tile + 1) % tiles]
            centre.append(s_ref[base + k, tile].astype(F32))
            edge.append(jnp.where(left_half, after, before).astype(F32))
        taps = []
        for b in range(4):
            shift = first + b
            outside = (lane < shift) | (lane >= LANES + shift)
            taps.append((outside, (LANES - shift) & (LANES - 1)))
        result = []
        for i in range(BLOCK_ROWS):
            c = sum(wr[a] * centre[i + a] for a in range(4))
            e = sum(wr[a] * edge[i + a] for a in range(4))
            total = None
            for b in range(4):
                outside, turn = taps[b]
                term = wc[b] * pltpu.roll(jnp.where(outside, e, c), turn, 1)
                total = term if total is None else total + term
            result.append(total)
        return result

    for band in range(bands):
        for tile in range(5 if last else 6):
            if tile < 5:
                dep = departed(band, tile, tile)
            else:
                right = departed(band, 5, tile)
                left = departed(band, -1, tile)
                dep = [jnp.where(left_half, r, l) for r, l in zip(right, left)]
            low = jnp.concatenate(dep, axis=1).astype(BF16)
            forcing = jnp.dot(phys, low, preferred_element_type=F32)
            for i in range(BLOCK_ROWS):
                push = forcing[:, i * LANES : (i + 1) * LANES] + bias
                value = dep[i] + jnp.tanh(push)
                row = band * BLOCK_ROWS + i
                if last:
                    refs[1][row, tile] = value
                else:
                    refs[0][row, tile] = value.astype(BF16)
    if not last:
        send_rows(refs[0], rows - ABOVE, refs[1])
        send_rows(refs[0], 0, refs[2])
    if last:
        for t in range(5):
            for g in range(0, fields, 8):
                got = jnp.swapaxes(refs[1][:, t, pl.ds(g, 8), :], 0, 1)
                refs[0][pl.ds(g, 8), :, pl.ds(t * LANES, LANES)] = got.astype(BF16)


def advance(last, params, before, now, after, phys, bias, *edges):
    rows, tiles, fields = now.shape[:3]
    anywhere, vmem = pl.BlockSpec(memory_space=pl.ANY), pl.BlockSpec(memory_space=pltpu.VMEM)
    scratch = [pltpu.VMEM((ABOVE + rows + BELOW, tiles, fields, LANES), BF16)]
    scratch += [pltpu.SMEM(params.shape, F32), pltpu.SMEM((2, LANES), F32), pltpu.SemaphoreType.DMA((2,))]
    if last:
        shape = jax.ShapeDtypeStruct((fields, rows, 5 * LANES), BF16)
        scratch.insert(0, pltpu.VMEM((rows, 5, fields, LANES), F32))
    else:
        shape = state_shapes(rows, tiles, fields)
    return pl.pallas_call(
        functools.partial(advance_kernel, last),
        out_shape=shape,
        in_specs=[anywhere] + [vmem] * 5 + [anywhere] * len(edges),
        scratch_shapes=scratch,
        compiler_params=pltpu.CompilerParams(vmem_limit_bytes=16 << 20),
        name="advance_last" if last else "advance_first",
    )(params, before, now, after, phys, bias, *edges)


def row_halos(last, first):
    size = lax.axis_size("wave")
    before = lax.ppermute(last, "wave", [(i, i + 1) for i in range(size - 1)])
    after = lax.ppermute(first, "wave", [(i + 1, i) for i in range(size - 1)])
    return before, after


def shards(spectral, wave_ids, lat_rows, shift_rows, shift_cols, frac_rows, frac_cols, phys_weight, phys_bias):
    slots, parts, fields, waves = spectral.shape
    lats = lat_rows.shape[0]
    bands, owners = lax.axis_size("wave"), lax.axis_size("lev")
    nlon = shift_rows.shape[2] * BLOCK_COLS * owners
    scale = 1.0 / math.sqrt(waves)
    outgoing = legendre(
        spectral, wave_ids, lat_rows, 8 * lats, nlon // owners - 1, 2 * nlon, scale
    )
    outgoing = outgoing.reshape(bands, lats // bands, slots * parts * fields)
    arrived = lax.all_to_all(outgoing, "wave", split_axis=0, concat_axis=0, tiled=True)
    table, m, stamp, params = fourier_table(
        wave_ids[None, :], shift_rows, shift_cols, frac_rows, frac_cols, 2 * nlon, 6
    )
    bias = phys_bias[None, :]
    arrived, params, bias = lax.optimization_barrier((arrived, params, bias))
    columns = fourier(arrived, m, stamp, table, scale)
    columns = lax.all_to_all(columns, "lev", split_axis=0, concat_axis=0, tiled=True)
    state, last, first, edges = regroup(columns)
    before, after = row_halos(last, first)
    state, last, first = advance(False, params, before, state, after, phys_weight, bias, edges)
    before, after = row_halos(last, first)
    return advance(True, params, before, state, after, phys_weight, bias)


def solution(mesh):
    blocks = P(None, "wave", "lev")
    return jax.shard_map(
        shards,
        mesh=mesh,
        in_specs=(P("wave", None, "lev", None), P(), P(), blocks, blocks, blocks, blocks, P(), P()),
        out_specs=P(None, "wave", "lev"),
        check_vma=False,
    )
```
